32 devices in a mesh: dp: 16 (over z, y, x), pair: 2 (over core).
Axes of the slice: x: 2, y: 2, z: 4, core: 2. Of those that a mesh axis runs over, the one named last changes fastest.
Arguments:
- tokens: bfloat16 [16384, 768], P(('dp', 'pair')), may hold values from -6 to 6
- span_starts: int32 [32, 14], P(('dp', 'pair')), may hold values from 1 to 501
- span_lengths: int32 [32, 14], P(('dp', 'pair')), may hold values from 1 to 10
- mask_embed: bfloat16 [768], replicated, may hold values from -6 to 6
- query_weight: bfloat16 [768, 768], P(('dp', 'pair')), may hold values from -0.21875 to 0.21875
- key_weight: bfloat16 [768, 768], P(('dp', 'pair')), may hold values from -0.21875 to 0.21875
- value_weight: bfloat16 [768, 768], P(('dp', 'pair')), may hold values from -0.21875 to 0.21875
- output_weight: bfloat16 [768, 768], P(('dp', 'pair')), may hold values from -0.875 to 0.875
- inner_weight: bfloat16 [768, 3072], P(('dp', 'pair')), may hold values from -0.21875 to 0.21875
- outer_weight: bfloat16 [3072, 768], P(('dp', 'pair')), may hold values from -0.109375 to 0.109375
- query_bias: float32 [768], replicated, may hold values from -3 to 3
- value_bias: float32 [768], replicated, may hold values from -3 to 3
- output_bias: float32 [768], replicated, may hold values from -3 to 3
- inner_bias: float32 [3072], replicated, may hold values from -3 to 3
- outer_bias: float32 [768], replicated, may hold values from -3 to 3
- gain_one: float32 [768], replicated, may hold values from 0.5 to 1.5
- shift_one: float32 [768], replicated, may hold values from -3 to 3
- gain_two: float32 [768], replicated, may hold values from 0.5 to 1.5
- shift_two: float32 [768], replicated, may hold values from -3 to 3
- cotangent: bfloat16 [16384, 768], P(('dp', 'pair')), may hold values from -6 to 6
Outputs:
- layer_output: bfloat16 [16384, 768], P(('dp', 'pair'))
- input_grad: bfloat16 [16384, 768], P(('dp', 'pair'))
- query_grad: float32 [768, 768], P(('dp', 'pair'))
- key_grad: float32 [768, 768], P(('dp', 'pair'))
- value_grad: float32 [768, 768], P(('dp', 'pair'))
- output_grad: float32 [768, 768], P(('dp', 'pair'))
- inner_grad: float32 [768, 3072], P(('dp', 'pair'))
- outer_grad: float32 [3072, 768], P(('dp', 'pair'))
- query_bias_grad: float32 [768], replicated
- value_bias_grad: float32 [768], replicated
- output_bias_grad: float32 [768], replicated
- inner_bias_grad: float32 [3072], replicated
- outer_bias_grad: float32 [768], replicated
- gain_one_grad: float32 [768], replicated
- shift_one_grad: float32 [768], replicated
- gain_two_grad: float32 [768], replicated
- shift_two_grad: float32 [768], replicated
- mask_grad: float32 [768], replicated
The draws below stay inside these ranges and needn't reach their ends.
Inputs may be any that keep to these rules, and one draw needn't show every extreme that they name: `span_starts`: each span and its two boundary positions lie inside its sequence; spans may intersect.
All inputs are finite; a program needn't handle non-finite values.
Results may differ from the reference program's by a relative error of at most 0.014.
Values may be sent and summed in bfloat16 or wider, within the bound.
No kernel may reach another device: no remote copies, remote signals or barrier semaphores. Data moves between devices by JAX's collectives and lax.ppermute only.
A program may use at most 192 MiB of HBM per device.

```python
import jax
import jax.numpy as jnp
from jax import lax

D = 768
FF = 3072
H = 12
HD = 64
LEN = 512
SPAN_MAX = 10
NSPAN = 14
SEQS = 32
TOKENS = 16384


def touch_ends(array, rng, smallest, largest):
    index_at = [jax.random.randint(jax.random.fold_in(rng, axis), (), 0, length) for axis, length in enumerate(array.shape)]
    longest = array.shape.index(max(array.shape))
    beside = index_at[:longest] + [(index_at[longest] + 1) % array.shape[longest]] + index_at[longest + 1:]
    return array.at[tuple(index_at)].set(smallest).at[tuple(beside)].set(largest)


def shard_levels(stream_key, extent, shards, smallest, high):
    loudness, own = 1.0, jax.random.fold_in(stream_key, 6)
    for axis_at, shards_of in shards:
        draws = jnp.exp(jax.random.uniform(jax.random.fold_in(own, axis_at), (shards_of,), jnp.float32, smallest / len(shards), high / len(shards)))
        loudness = loudness * jnp.repeat(draws, extent[axis_at] // shards_of).reshape([-1 if axis == axis_at else 1 for axis in range(len(extent))])
    return loudness


def normal_values(stream_key, dims, scale, reach, shards=(), held_as=jnp.bfloat16):
    drawn = scale * jax.random.normal(stream_key, dims, jnp.float32)
    if shards:
        drawn = drawn * shard_levels(stream_key, dims, shards, -0.22, 0.18)
    return jnp.clip(drawn, -reach, reach).astype(held_as)


def setup_inputs(seed: int = 0) -> dict:
    splits = jax.random.split(jax.random.key(seed), 21)
    return {
        "tokens": normal_values(splits[0], (TOKENS, D), 1.0, 6.0, ((0, 32),)),
        "span_starts": touch_ends(jax.random.randint(splits[1], (SEQS, NSPAN), 1, LEN - SPAN_MAX), jax.random.fold_in(splits[1], 1), 1, (LEN - SPAN_MAX) - 1).astype(jnp.int32),
        "span_lengths": touch_ends(jax.random.randint(splits[2], (SEQS, NSPAN), 1, SPAN_MAX + 1), jax.random.fold_in(splits[2], 1), 1, SPAN_MAX).astype(jnp.int32),
        "mask_embed": normal_values(splits[3], (D,), 1.0, 6.0),
        "query_weight": normal_values(splits[4], (D, D), D ** -0.5, 0.21875, ((0, 32),)),
        "key_weight": normal_values(splits[5], (D, D), D ** -0.5, 0.21875, ((0, 32),)),
        "value_weight": normal_values(splits[6], (D, D), D ** -0.5, 0.21875, ((0, 32),)),
        "output_weight": normal_values(splits[7], (D, D), (D // 16) ** -0.5, 0.875, ((0, 32),)),
        "inner_weight": normal_values(splits[8], (D, FF), D ** -0.5, 0.21875, ((0, 32),)),
        "outer_weight": normal_values(splits[9], (FF, D), FF ** -0.5, 0.109375, ((0, 32),)),
        "query_bias": normal_values(splits[10], (D,), 0.5, 3.0, (), jnp.float32),
        "value_bias": normal_values(splits[11], (D,), 0.5, 3.0, (), jnp.float32),
        "output_bias": normal_values(splits[12], (D,), 0.5, 3.0, (), jnp.float32),
        "inner_bias": normal_values(splits[13], (FF,), 0.5, 3.0, (), jnp.float32),
        "outer_bias": normal_values(splits[14], (D,), 0.5, 3.0, (), jnp.float32),
        "gain_one": jnp.clip(1.0 + 0.1 * jax.random.normal(splits[15], (D,), jnp.float32), 0.5, 1.5),
        "shift_one": normal_values(splits[16], (D,), 0.5, 3.0, (), jnp.float32),
        "gain_two": jnp.clip(1.0 + 0.1 * jax.random.normal(splits[17], (D,), jnp.float32), 0.5, 1.5),
        "shift_two": normal_values(splits[18], (D,), 0.5, 3.0, (), jnp.float32),
        "cotangent": normal_values(splits[19], (TOKENS, D), 1.0, 6.0, ((0, 32),)),
    }


@jax.custom_vjp
def low(v):
    return lax.optimization_barrier(v.astype(jnp.bfloat16)).astype(jnp.float32)

@jax.custom_vjp
def low_back(v):
    return v

def low_keep(v):
    return (low(v), None)

def low_pass(kept, grad):
    return (grad,)

def back_keep(v):
    return (v, None)

def back_low(kept, grad):
    return (low(grad),)
low.defvjp(low_keep, low_pass)
low_back.defvjp(back_keep, back_low)

def matmul(left, right):
    return jnp.dot(left, right, precision=lax.Precision.HIGHEST)

def layer_norm(value, gain, shift):
    centered = value - lax.optimization_barrier(jnp.mean(value, axis=-1, keepdims=True))
    spread = lax.optimization_barrier(jnp.mean(centered * centered, axis=-1, keepdims=True))
    return centered * lax.rsqrt(spread + 1e-12) * gain + shift

def span_masks(span_starts, span_lengths):
    places = jnp.arange(LEN, dtype=jnp.int32)[None, :, None]
    begins = span_starts[:, None, :]
    finish = begins + span_lengths[:, None, :]
    masked = jnp.any((places >= begins) & (places < finish), axis=2)
    edges = jnp.any((places == begins - 1) | (places == finish), axis=2)
    return (masked, masked | edges)

def attend(triple):
    query, key, value = triple
    query = query.reshape(LEN, H, HD)
    key = key.reshape(LEN, H, HD)
    value = value.reshape(LEN, H, HD)
    scores = jnp.einsum('qhd,khd->hqk', query, key, precision=lax.Precision.HIGHEST) * HD ** (-0.5)
    scores = low_back(scores)
    probs = low(jax.nn.softmax(scores, axis=-1))
    context = jnp.einsum('hqk,khd->qhd', probs, value, precision=lax.Precision.HIGHEST)
    return context.reshape(LEN, H * HD)

def forward(params, embed, inputs, masked):
    query_weight, key_weight, value_weight, output_weight, inner_weight, outer_weight, query_bias, value_bias, output_bias, inner_bias, outer_bias, gain_one, shift_one, gain_two, shift_two = params
    start = jnp.where(masked[:, None], embed[None, :], inputs)
    start_low = low(start)
    query = low(low_back(matmul(start_low, query_weight) + query_bias))
    key = low(low_back(matmul(start_low, key_weight)))
    value = low(low_back(matmul(start_low, value_weight) + value_bias))
    count = inputs.shape[0] // LEN
    context = lax.map(jax.checkpoint(attend), (query.reshape(count, LEN, H * HD), key.reshape(count, LEN, H * HD), value.reshape(count, LEN, H * HD)))
    context = low(low_back(context.reshape(count * LEN, H * HD)))
    attended = low_back(matmul(context, output_weight) + output_bias)
    first = start + attended
    normed = layer_norm(first, gain_one, shift_one)
    hidden = low_back(matmul(low(normed), inner_weight) + inner_bias)
    active = low(jax.nn.gelu(hidden, approximate=False))
    branch = low_back(matmul(active, outer_weight) + outer_bias)
    return layer_norm(normed + branch, gain_two, shift_two)

def reference(tokens, span_starts, span_lengths, mask_embed, query_weight, key_weight, value_weight, output_weight, inner_weight, outer_weight, query_bias, value_bias, output_bias, inner_bias, outer_bias, gain_one, shift_one, gain_two, shift_two, cotangent):
    masked, wanted = span_masks(span_starts, span_lengths)
    params = tuple((w.astype(jnp.float32) for w in (query_weight, key_weight, value_weight, output_weight, inner_weight, outer_weight, query_bias, value_bias, output_bias, inner_bias, outer_bias, gain_one, shift_one, gain_two, shift_two)))
    embed = mask_embed.astype(jnp.float32)
    seqs = span_starts.shape[0]
    groups = seqs // 8
    width = tokens.shape[1]
    inputs = tokens.astype(jnp.float32).reshape(groups, 8 * LEN, width)
    grads_in = cotangent.astype(jnp.float32).reshape(groups, 8 * LEN, width)
    mask_rows = masked.reshape(groups, 8 * LEN)
    want_rows = wanted.reshape(groups, 8 * LEN)

    def step(carry, item):
        block, mask_block, want_block, grad_block = item

        def local(p, e, x):
            return forward(p, e, x, mask_block)
        result, backward = jax.vjp(local, params, embed, block)
        param_grads, embed_grad, input_grads = backward(grad_block * want_block[:, None].astype(jnp.float32))
        carry = (jax.tree.map(lambda a, b: a + b, carry[0], param_grads), carry[1] + embed_grad)
        return (carry, (result.astype(jnp.bfloat16), input_grads.astype(jnp.bfloat16)))
    start = (jax.tree.map(jnp.zeros_like, params), jnp.zeros_like(embed))
    (param_grads, embed_grad), (results, input_grads) = lax.scan(step, start, (inputs, mask_rows, want_rows, grads_in))
    total = seqs * LEN
    return (results.reshape(total, width), input_grads.reshape(total, width), param_grads[0], param_grads[1], param_grads[2], param_grads[3], param_grads[4], param_grads[5], param_grads[6], param_grads[7], param_grads[8], param_grads[9], param_grads[10], param_grads[11], param_grads[12], param_grads[13], param_grads[14], embed_grad)
```

```python
import jax
import jax.numpy as jnp
from jax import lax
from jax.sharding import PartitionSpec as P

HD = 64


def layer_norm(value, gain, shift):
    centered = value - jnp.mean(value, axis=-1, keepdims=True)
    spread = jnp.mean(centered * centered, axis=-1, keepdims=True)
    return centered * lax.rsqrt(spread + 1e-12) * gain + shift


def gelu_exact(value):
    return jax.nn.gelu(value, approximate=False)


def dense(left, right):
    return jnp.dot(left, right, preferred_element_type=jnp.float32)


def outer_sum(left, right):
    return jnp.einsum("rd,re->de", left, right, preferred_element_type=jnp.float32)


def back_dense(grad, weight):
    return jnp.einsum("re,de->rd", grad, weight, preferred_element_type=jnp.float32)


def grid_of(count):
    fast = 1
    while fast * fast * fast * 2 <= count:
        fast *= 2
    return (count // (fast * fast), fast, fast)


class Place:
    def __init__(self):
        self.sizes = grid_of(lax.axis_size("dp"))
        index = lax.axis_index("dp")
        slow, mid, fast = self.sizes
        self.at = {
            "s": index // (mid * fast),
            "m": index // fast % mid,
            "f": index % fast,
            "c": lax.axis_index("pair"),
        }
        self.n = {"s": slow, "m": mid, "f": fast, "c": lax.axis_size("pair")}

    def shift(self, value, part, step):
        size = self.n[part]
        if part == "c":
            return lax.ppermute(value, "pair", [(i, (i + step) % size) for i in range(size)])
        slow, mid, fast = self.sizes
        pairs = []
        for s in range(slow):
            for m in range(mid):
                for f in range(fast):
                    to = {"s": s, "m": m, "f": f}
                    to[part] = (to[part] + step) % size
                    pairs.append(
                        ((s * mid + m) * fast + f, (to["s"] * mid + to["m"]) * fast + to["f"])
                    )
        return lax.ppermute(value, "dp", pairs)

    def spread(self, value, part):
        size, at = self.n[part], self.at[part]
        got = [value] + [self.shift(value, part, k) for k in range(1, size)]
        rows = []
        for j in range(size):
            row = got[0]
            for k in range(1, size):
                row = jnp.where((at - j) % size == k, got[k], row)
            rows.append(row)
        return jnp.stack(rows)

    def collect(self, value, part, axis, final=False):
        size, at = self.n[part], self.at[part]
        take = lambda j: lax.dynamic_index_in_dim(value, j, axis, keepdims=False)
        total = take(at).astype(jnp.float32)
        for k in range(1, size):
            total = total + self.shift(take((at + k) % size), part, k).astype(jnp.float32)
        return total if final else total.astype(jnp.bfloat16)


def gather_two(place, left, right):
    done = []
    left, right = place.spread(left, "s"), place.spread(right, "s")
    left, right = place.spread(left, "m"), place.spread(right, "f")
    left, right = place.spread(left, "f"), place.spread(right, "m")
    left, right = place.spread(left, "c"), place.spread(right, "c")
    left = left.transpose(3, 2, 1, 0, 4, 5)
    right = right.transpose(3, 1, 2, 0, 4, 5)
    return left.reshape(-1, left.shape[-1]), right.reshape(-1, right.shape[-1])


def scatter_two(place, left, right):
    n = place.n
    shape = lambda v: v.reshape(n["s"], n["m"], n["f"], n["c"], -1, v.shape[-1])
    left, right = shape(left), shape(right)
    left, right = place.collect(left, "c", 3), place.collect(right, "c", 3)
    left, right = place.collect(left, "f", 2), place.collect(right, "m", 1)
    left, right = place.collect(left, "m", 1), place.collect(right, "f", 1)
    left, right = place.collect(left, "s", 0, True), place.collect(right, "s", 0, True)
    return left, right


def total_of(place, value):
    for part in ("c", "f", "m", "s"):
        size, at = place.n[part], place.at[part]
        step = 1
        while step < size:
            if part == "c":
                got = lax.ppermute(value, "pair", [(i, i ^ step) for i in range(size)])
            else:
                slow, mid, fast = place.sizes
                stride = {"s": mid * fast, "m": fast, "f": 1}[part] * step
                got = lax.ppermute(value, "dp", [(i, i ^ stride) for i in range(slow * mid * fast)])
            value = value + got
            step *= 2
    return value


def on_device(
    tokens,
    span_starts,
    span_lengths,
    mask_embed,
    query_weight,
    key_weight,
    value_weight,
    output_weight,
    inner_weight,
    outer_weight,
    query_bias,
    value_bias,
    output_bias,
    inner_bias,
    outer_bias,
    gain_one,
    shift_one,
    gain_two,
    shift_two,
    cotangent,
):
    rows, width = tokens.shape
    seqs = span_starts.shape[0]
    length = rows // seqs
    heads = width // HD
    factor = HD ** (-0.5)
    places = jnp.arange(length, dtype=jnp.int32)[None, :, None]
    begins = span_starts[:, None, :]
    finish = begins + span_lengths[:, None, :]
    masked = jnp.any((places >= begins) & (places < finish), axis=2)
    edges = jnp.any((places == begins - 1) | (places == finish), axis=2)
    masked = masked.reshape(rows)
    wanted = (masked | edges.reshape(rows)).astype(jnp.float32)
    start = jnp.where(masked[:, None], mask_embed[None, :], tokens)
    place = Place()
    half, inner_half = width // 2, inner_weight.shape[1] // 2
    triple = (query_weight, key_weight, value_weight)
    qkv_left, qkv_right = gather_two(
        place,
        jnp.concatenate([w[:, :half] for w in triple], axis=1),
        jnp.concatenate([w[:, half:] for w in triple], axis=1),
    )
    in_left, in_right = gather_two(
        place,
        jnp.concatenate([output_weight[:, :half], inner_weight[:, :inner_half]], axis=1),
        jnp.concatenate([output_weight[:, half:], inner_weight[:, inner_half:]], axis=1),
    )
    wu = jnp.concatenate(
        gather_two(place, outer_weight[:, :half], outer_weight[:, half:]), axis=1
    )
    wq, wk, wv = (
        jnp.concatenate([qkv_left[:, i * half : (i + 1) * half], qkv_right[:, i * half : (i + 1) * half]], axis=1)
        for i in range(3)
    )
    wo = jnp.concatenate([in_left[:, :half], in_right[:, :half]], axis=1)
    wi = jnp.concatenate([in_left[:, half:], in_right[:, half:]], axis=1)
    query = (dense(start, wq) + query_bias).astype(jnp.bfloat16)
    key = dense(start, wk).astype(jnp.bfloat16)
    value = (dense(start, wv) + value_bias).astype(jnp.bfloat16)
    query4 = query.reshape(seqs, length, heads, HD)
    key4 = key.reshape(seqs, length, heads, HD)
    value4 = value.reshape(seqs, length, heads, HD)
    scores = (
        jnp.einsum("sqhd,skhd->shqk", query4, key4, preferred_element_type=jnp.float32) * factor
    )
    lse = jax.nn.logsumexp(scores, axis=-1, keepdims=True)
    probs = jnp.exp(scores - lse).astype(jnp.bfloat16)
    context = jnp.einsum("shqk,skhd->sqhd", probs, value4, preferred_element_type=jnp.float32)
    context = context.reshape(rows, width).astype(jnp.bfloat16)
    first = start.astype(jnp.float32) + dense(context, wo) + output_bias
    normed = layer_norm(first, gain_one, shift_one)
    normed_low = normed.astype(jnp.bfloat16)
    hidden = dense(normed_low, wi) + inner_bias
    active = gelu_exact(hidden).astype(jnp.bfloat16)
    second = normed + dense(active, wu) + outer_bias
    layer_output = layer_norm(second, gain_two, shift_two).astype(jnp.bfloat16)
    grad_out = cotangent.astype(jnp.float32) * wanted[:, None]
    norm_two, norm_two_back = jax.vjp(layer_norm, second, gain_two, shift_two)
    grad_second, gain_two_grad, shift_two_grad = norm_two_back(grad_out)
    grad_branch = grad_second.astype(jnp.bfloat16)
    outer_bias_grad = jnp.sum(grad_branch.astype(jnp.float32), axis=0)
    outer_grad = outer_sum(active, grad_branch)
    grad_active = back_dense(grad_branch, wu)
    gelu_value, gelu_back = jax.vjp(gelu_exact, hidden)
    grad_hidden = gelu_back(grad_active)[0].astype(jnp.bfloat16)
    inner_bias_grad = jnp.sum(grad_hidden.astype(jnp.float32), axis=0)
    inner_grad = outer_sum(normed_low, grad_hidden)
    grad_normed = grad_second + back_dense(grad_hidden, wi)
    norm_one, norm_one_back = jax.vjp(layer_norm, first, gain_one, shift_one)
    grad_first, gain_one_grad, shift_one_grad = norm_one_back(grad_normed)
    grad_attended = grad_first.astype(jnp.bfloat16)
    output_bias_grad = jnp.sum(grad_attended.astype(jnp.float32), axis=0)
    output_grad = outer_sum(context, grad_attended)
    grad_context = back_dense(grad_attended, wo).astype(jnp.bfloat16)
    grad_context4 = grad_context.reshape(seqs, length, heads, HD)
    scores = (
        jnp.einsum("sqhd,skhd->shqk", query4, key4, preferred_element_type=jnp.float32) * factor
    )
    fresh = jnp.exp(scores - lse)
    fresh_low = fresh.astype(jnp.bfloat16)
    grad_probs = jnp.einsum(
        "sqhd,skhd->shqk", grad_context4, value4, preferred_element_type=jnp.float32
    )
    grad_value = jnp.einsum(
        "shqk,sqhd->skhd", fresh_low, grad_context4, preferred_element_type=jnp.float32
    )
    grad_scores = fresh * (grad_probs - jnp.sum(fresh * grad_probs, axis=-1, keepdims=True))
    grad_scores = grad_scores.astype(jnp.bfloat16)
    grad_query = (
        jnp.einsum("shqk,skhd->sqhd", grad_scores, key4, preferred_element_type=jnp.float32)
        * factor
    )
    grad_key = (
        jnp.einsum("shqk,sqhd->skhd", grad_scores, query4, preferred_element_type=jnp.float32)
        * factor
    )
    grad_query = grad_query.reshape(rows, width).astype(jnp.bfloat16)
    grad_key = grad_key.reshape(rows, width).astype(jnp.bfloat16)
    grad_value = grad_value.reshape(rows, width).astype(jnp.bfloat16)
    query_bias_grad = jnp.sum(grad_query.astype(jnp.float32), axis=0)
    value_bias_grad = jnp.sum(grad_value.astype(jnp.float32), axis=0)
    query_grad = outer_sum(start, grad_query)
    key_grad = outer_sum(start, grad_key)
    value_grad = outer_sum(start, grad_value)
    grad_start = (
        grad_first
        + back_dense(grad_query, wq)
        + back_dense(grad_key, wk)
        + back_dense(grad_value, wv)
    )
    input_grad = jnp.where(masked[:, None], 0.0, grad_start).astype(jnp.bfloat16)
    mask_grad = jnp.sum(jnp.where(masked[:, None], grad_start, 0.0), axis=0)
    low = jnp.bfloat16
    outer_rows = scatter_two(
        place, outer_grad[:, :half].astype(low), outer_grad[:, half:].astype(low)
    )
    inner_rows = scatter_two(
        place, inner_grad[:, :inner_half].astype(low), inner_grad[:, inner_half:].astype(low)
    )
    four = [g.astype(low) for g in (query_grad, key_grad, value_grad, output_grad)]
    four_rows = scatter_two(
        place,
        jnp.concatenate(four[:2], axis=1),
        jnp.concatenate(four[2:], axis=1),
    )
    smalls = (
        query_bias_grad,
        value_bias_grad,
        output_bias_grad,
        inner_bias_grad,
        outer_bias_grad,
        gain_one_grad,
        shift_one_grad,
        gain_two_grad,
        shift_two_grad,
        mask_grad,
    )
    packed = total_of(place, jnp.concatenate(smalls).reshape(-1, 128)).reshape(-1)
    ends = [0]
    for value in smalls:
        ends.append(ends[-1] + value.shape[0])
    return (
        layer_output,
        input_grad,
        four_rows[0][:, :width],
        four_rows[0][:, width:],
        four_rows[1][:, :width],
        four_rows[1][:, width:],
        jnp.concatenate(inner_rows, axis=1),
        jnp.concatenate(outer_rows, axis=1),
        *(packed[a:b] for a, b in zip(ends[:-1], ends[1:])),
    )


def solution(mesh):
    placed = (
        P(("dp", "pair"), None),
        P(("dp", "pair"), None),
        P(("dp", "pair"), None),
        P(),
        P(("dp", "pair"), None),
        P(("dp", "pair"), None),
        P(("dp", "pair"), None),
        P(("dp", "pair"), None),
        P(("dp", "pair"), None),
        P(("dp", "pair"), None),
        P(),
        P(),
        P(),
        P(),
        P(),
        P(),
        P(),
        P(),
        P(),
        P(("dp", "pair"), None),
    )
    return jax.shard_map(
        on_device,
        mesh=mesh,
        in_specs=placed,
        out_specs=(
            P(("dp", "pair"), None),
            P(("dp", "pair"), None),
            P(("dp", "pair"), None),
            P(("dp", "pair"), None),
            P(("dp", "pair"), None),
            P(("dp", "pair"), None),
            P(("dp", "pair"), None),
            P(("dp", "pair"), None),
            P(),
            P(),
            P(),
            P(),
            P(),
            P(),
            P(),
            P(),
            P(),
            P(),
        ),
        check_vma=False,
    )
```

```python
import jax
import jax.numpy as jnp
from jax import lax
from jax.experimental import pallas as pl
from jax.experimental.pallas import tpu as pltpu
from jax.sharding import PartitionSpec as P

HD = 64
BOTH = ("dp", "pair")
LOW = jnp.bfloat16


def hold(value, *others):
    others = [o for o in others if o is not None]
    return lax.optimization_barrier((value, *others))[0] if others else value


class Place:
    def __init__(self):
        self.chips = lax.axis_size("dp")
        fast = 1
        while (2 * fast) ** 3 <= self.chips:
            fast *= 2
        strides = []
        while (1 << len(strides)) < self.chips:
            strides.insert(0, self.chips >> (len(strides) + 1))
        strides = sorted(strides, reverse=True)
        self.fast = [b for b in strides if b < fast]
        self.mid = [b for b in strides if fast <= b < fast * fast]
        self.slow = [b for b in strides if b >= fast * fast]
        self.chip = lax.axis_index("dp")
        self.core = lax.axis_index("pair")
        self.where = jnp.stack([self.chip, self.core]).astype(jnp.int32)

    def swap(self, value, stride):
        return lax.ppermute(value, "dp", [(i, i ^ stride) for i in range(self.chips)])

    def swap_core(self, value):
        return lax.ppermute(value, "pair", [(0, 1), (1, 0)])


def kernel_call(body, grid, in_specs, out_specs, out_shape, cost, scratch=(), limit=None):
    flops, moved, special = cost
    return pl.pallas_call(
        body,
        grid_spec=pltpu.PrefetchScalarGridSpec(
            num_scalar_prefetch=1,
            grid=grid,
            in_specs=in_specs,
            out_specs=out_specs,
            scratch_shapes=scratch,
        ),
        out_shape=out_shape,
        cost_estimate=pl.CostEstimate(
            flops=flops, bytes_accessed=moved, transcendentals=special
        ),
        compiler_params=pltpu.CompilerParams(vmem_limit_bytes=limit or 32 * 2**20),
    )


def pack(place, arrays, spots, shape):
    def body(at, *refs):
        out = refs[-1]
        for i, begin, width, row, column in spots:
            value = refs[i][:, begin : begin + width]
            out[row : row + value.shape[0], column : column + width] = value

    moved = 2 * sum(a.size * a.dtype.itemsize for a in arrays)
    return kernel_call(
        body,
        (1,),
        [pl.BlockSpec(a.shape, lambda i, at: (0, 0)) for a in arrays],
        pl.BlockSpec(shape, lambda i, at: (0, 0)),
        jax.ShapeDtypeStruct(shape, arrays[0].dtype),
        (0, moved, 0),
    )(place.where, *arrays)


class Gather:
    def __init__(self, place, rows):
        self.place = place
        self.slots = rows[None]
        self.left = place.slow + place.mid + place.fast
        self.right = place.slow + place.fast + place.mid
        self.stage = 0
        self.halves = None

    def step(self, before=(), during=()):
        place, stage = self.place, self.stage
        self.stage += 1
        if stage < len(place.slow):
            value = hold(self.slots, *before)
            got = hold(place.swap(value, self.left[stage]), *during)
            self.slots = jnp.concatenate([value, got])
            return got
        if stage < len(self.left):
            if self.halves is None:
                half = self.slots.shape[-1] // 2
                self.halves = (self.slots[..., :half], self.slots[..., half:])
            l, r = (hold(v, *before) for v in self.halves)
            gl = hold(place.swap(l, self.left[stage]), *during)
            gr = hold(place.swap(r, self.right[stage]), *during)
            self.halves = (jnp.concatenate([l, gl]), jnp.concatenate([r, gr]))
            return gr
        self.own = hold(jnp.stack(self.halves), *before)
        self.other = hold(place.swap_core(self.own), *during)
        return self.other

    def done(self, parts):
        place = self.place
        _, chips, rows, half = self.own.shape
        orders = (self.left, self.right)

        def body(at, own, other, *outs):
            chip, core = at[0], at[1]
            for side in range(2):

                def put(j, carry):
                    to = chip
                    for i, stride in enumerate(orders[side]):
                        to = to ^ (((j >> i) & 1) * stride)
                    begin = 0
                    for out, width in zip(outs, parts):
                        cols = slice(side * width, (side + 1) * width)
                        out[2 * to + core, :, cols] = own[side, j, :, begin : begin + width]
                        out[2 * to + 1 - core, :, cols] = other[side, j, :, begin : begin + width]
                        begin += width
                    return carry

                lax.fori_loop(0, chips, put, 0)

        moved = 8 * chips * rows * half * 2
        whole = pl.BlockSpec((2, chips, rows, half), lambda i, at: (0, 0, 0, 0))
        outs = kernel_call(
            body,
            (1,),
            [whole, whole],
            [pl.BlockSpec((2 * chips, rows, 2 * w), lambda i, at: (0, 0, 0)) for w in parts],
            [jax.ShapeDtypeStruct((2 * chips, rows, 2 * w), LOW) for w in parts],
            (0, moved, 0),
        )(place.where, self.own, self.other)
        return [o.reshape(-1, o.shape[-1]) for o in outs]


def fold(place, keeps, gots, bits, join):
    sides = len(bits)
    deep = keeps[0].ndim == 4
    chips, rows, cols = keeps[0].shape[-3:]
    steps = next(s for s in (3, 2, 1) if rows % (8 * s) == 0)
    part = rows // steps

    def body(at, *refs):
        ins, outs = refs[: 2 * len(keeps)], refs[2 * len(keeps) :]
        for side in range(sides):
            for j in range(chips):
                if deep:
                    a, b = ins[0][side, j], ins[1][side, j]
                else:
                    a, b = ins[side][j], ins[len(keeps) + side][j]
                total = (a.astype(jnp.float32) + b.astype(jnp.float32)).astype(LOW)
                low = bits[side]
                to = (j // (2 * low)) * low + j % low
                goes = (j // low) % 2
                if join:
                    outs[goes][to, :, side * cols : (side + 1) * cols] = total
                else:
                    outs[goes * sides + side][to] = total

    if deep:
        ins = pl.BlockSpec((2, chips, part, cols), lambda i, at: (0, 0, i, 0))
    else:
        ins = pl.BlockSpec((chips, part, cols), lambda i, at: (0, i, 0))
    wide = cols * sides if join else cols
    count = 2 if join else 2 * sides
    outs = kernel_call(
        body,
        (steps,),
        [ins] * (2 * len(keeps)),
        [pl.BlockSpec((chips // 2, part, wide), lambda i, at: (0, i, 0))] * count,
        [jax.ShapeDtypeStruct((chips // 2, rows, wide), LOW)] * count,
        (0, 6 * sides * chips * rows * cols, 0),
    )(place.where, *keeps, *gots)
    return list(outs[: count // 2]), list(outs[count // 2 :])


class Scatter:
    def __init__(self, place, keep, send):
        self.place = place
        self.keeps, self.sends = [keep], [send]
        self.left = (place.slow + place.mid + place.fast)[::-1]
        self.right = (place.slow + place.fast + place.mid)[::-1]
        self.held = [sorted(self.left), sorted(self.right)]
        self.stage = -1
        self.result = None
        self.gots = None

    def step(self, before=(), during=()):
        place = self.place
        if self.gots is not None:
            orders = (self.left, self.right)
            crossing = len(self.left) - len(place.slow)
            sides = 2 if self.stage <= crossing else 1
            bits = []
            for side in range(sides):
                stride = orders[side][self.stage]
                bits.append(1 << self.held[side].index(stride))
                self.held[side].remove(stride)
            join = self.stage == crossing
            self.keeps, self.sends = fold(place, self.keeps, self.gots, bits, join)
        swaps = (
            [place.swap_core]
            if self.stage < 0
            else [lambda v, b=o[self.stage]: place.swap(v, b) for o in (self.left, self.right)]
        )
        self.gots = [
            hold(swap(hold(v, *before)), *during) for v, swap in zip(self.sends, swaps)
        ]
        self.stage += 1
        if self.stage == len(self.left):
            self.result = self.keeps[0][0].astype(jnp.float32) + self.gots[0][0].astype(jnp.float32)
        return self.gots[-1]


def weight_terms(place, lefts, rights, rows):
    chips = place.chips
    count = len(lefts)
    length, features = lefts[0].shape
    joined = not isinstance(rights, list)
    width = rights.shape[1] // count if joined else rights[0].shape[1]
    per = count // 2
    unique = []
    for l in lefts:
        if not any(l is u for u in unique):
            unique.append(l)
    which = [next(i for i, u in enumerate(unique) if u is l) for l in lefts]
    rights = [rights] if joined else rights

    def body(at, *refs):
        ins, (keep, send) = refs[:-2], refs[-2:]
        t = pl.program_id(0)
        chip, core = at[0], at[1]

        def one(left, right):
            total = lax.dot_general(
                left[...], right[...], (((0,), (0,)), ((), ())), preferred_element_type=jnp.float32
            )
            for c in range(chips):
                to = c ^ chip
                a = total[2 * c * rows : (2 * c + 1) * rows].astype(LOW)
                b = total[(2 * c + 1) * rows : (2 * c + 2) * rows].astype(LOW)
                keep[0, to] = jnp.where(core == 0, a, b)
                send[0, to] = jnp.where(core == 0, b, a)

        if joined:
            one(ins[0], ins[1])
        else:
            for k in range(count):
                pl.when(t == k)(lambda k=k: one(ins[which[k]], ins[len(unique) + k]))

    block = pl.BlockSpec((1, chips, rows, width), lambda t, at: (t // per, 0, 0, t % per))
    shape = jax.ShapeDtypeStruct((2, chips, rows, width * per), LOW)
    fixed = pl.BlockSpec((length, width), lambda t, at: (0, 0))
    return kernel_call(
        body,
        (count,),
        [pl.BlockSpec((length, features), lambda t, at: (0, 0)) for _ in unique]
        + ([pl.BlockSpec((length, width), lambda t, at: (0, t))] if joined else [fixed] * count),
        [block, block],
        [shape, shape],
        (2 * count * length * features * width, 4 * count * features * width, 0),
    )(place.where, *unique, *rights)


def weight_terms_tall(place, left, right, rows):
    chips = place.chips
    length, features = left.shape
    width = right.shape[1]
    tiles = 4
    group = chips // tiles

    def body(at, left_ref, right_ref, keep, send):
        chip, core = at[0], at[1]
        total = lax.dot_general(
            left_ref[...], right_ref[...], (((0,), (0,)), ((), ())), preferred_element_type=jnp.float32
        )
        for c in range(group):
            to = c ^ (chip % group)
            a = total[2 * c * rows : (2 * c + 1) * rows].astype(LOW)
            b = total[(2 * c + 1) * rows : (2 * c + 2) * rows].astype(LOW)
            own, other = jnp.where(core == 0, a, b), jnp.where(core == 0, b, a)
            for side in range(2):
                cols = slice(side * (width // 2), (side + 1) * (width // 2))
                keep[side, to] = own[:, cols]
                send[side, to] = other[:, cols]

    block = pl.BlockSpec((2, group, rows, width // 2), lambda t, at: (0, t, 0, 0))
    shape = jax.ShapeDtypeStruct((2, chips, rows, width // 2), LOW)
    return kernel_call(
        body,
        (tiles,),
        [
            pl.BlockSpec((length, features // tiles), lambda t, at: (0, t ^ (at[0] // group))),
            pl.BlockSpec((length, width), lambda t, at: (0, 0)),
        ],
        [block, block],
        [shape, shape],
        (2 * length * features * width, 4 * features * width, 0),
    )(place.where, left, right)


class Total:
    def __init__(self, place, value):
        self.place, self.value = place, value
        self.strides = [0] + place.fast + place.mid + place.slow

    def step(self, before=(), during=()):
        value = hold(self.value, *before)
        stride = self.strides.pop(0)
        got = hold(self.place.swap(value, stride) if stride else self.place.swap_core(value), *during)
        self.value = value + got
        return got


def attention_forward(place, start, weights, query_bias, value_bias, seqs):
    rows, width = start.shape
    length = rows // seqs
    cols = 4 * HD
    groups = width // cols

    def body(at, start, wq, wk, wv, qb, vb, query, key, value, context, lse):
        x = start[...]
        dot = lambda l, r: jnp.dot(l, r, preferred_element_type=jnp.float32)
        query[...] = (dot(x, wq[...]) + qb[...]).astype(LOW)
        key[...] = dot(x, wk[...]).astype(LOW)
        value[...] = (dot(x, wv[...]) + vb[...]).astype(LOW)
        lane = lax.broadcasted_iota(jnp.int32, (length, 2 * HD), 1)
        for pair in range(2):
            at_cols = slice(pair * 2 * HD, (pair + 1) * 2 * HD)
            q, k = query[:, at_cols], key[:, at_cols]
            v_across = value[:, at_cols].T
            mixed = []
            for h in range(2):
                mine = (lane < HD) if h == 0 else (lane >= HD)
                q_mine = jnp.where(mine, q * jnp.asarray(HD**-0.5, LOW), jnp.zeros_like(q))
                scores = lax.dot_general(
                    k, q_mine, (((1,), (1,)), ((), ())), preferred_element_type=jnp.float32
                )
                most = jnp.max(scores, axis=0, keepdims=True)
                raised = jnp.exp(scores - most)
                total = jnp.sum(raised, axis=0, keepdims=True)
                probs = (raised * (1.0 / total)).astype(LOW)
                mixed.append(dot(v_across[h * HD : (h + 1) * HD], probs))
                lse[0, 0, 2 * pair + h : 2 * pair + h + 1, :] = most + jnp.log(total)
            context[:, at_cols] = jnp.concatenate(mixed, axis=0).T.astype(LOW)

    block = pl.BlockSpec((length, cols), lambda s, g, at: (s, g))
    weight = pl.BlockSpec((width, cols), lambda s, g, at: (0, g))
    bias = pl.BlockSpec((1, cols), lambda s, g, at: (0, g))
    table = jax.ShapeDtypeStruct((rows, width), LOW)
    return kernel_call(
        body,
        (seqs, groups),
        [pl.BlockSpec((length, width), lambda s, g, at: (s, 0)), weight, weight, weight, bias, bias],
        [block] * 4 + [pl.BlockSpec((1, 1, 4, length), lambda s, g, at: (s, g, 0, 0))],
        [table] * 4 + [jax.ShapeDtypeStruct((seqs, groups, 4, length), jnp.float32)],
        (6 * rows * width * width, 6 * width * width, seqs * groups * 4 * length * length),
    )(place.where, start, *weights, query_bias, value_bias)


def attention_backward(place, query, key, value, grad_context, lse):
    rows, width = query.shape
    seqs, groups, _, length = lse.shape
    cols = 4 * HD

    def body(at, query, key, value, grad, lse, dq, dk, dv, dq_sum, dv_sum):
        dot = lambda l, r: jnp.dot(l, r, preferred_element_type=jnp.float32)
        dot_t = lambda l, r: lax.dot_general(
            l, r, (((1,), (1,)), ((), ())), preferred_element_type=jnp.float32
        )
        lane = lax.broadcasted_iota(jnp.int32, (length, 2 * HD), 1)
        for pair in range(2):
            at_cols = slice(pair * 2 * HD, (pair + 1) * 2 * HD)
            q, k, v, g = query[:, at_cols], key[:, at_cols], value[:, at_cols], grad[:, at_cols]
            k_across = k.T
            dqs, dks, dvs = [], [], []
            for h in range(2):
                mine = (lane < HD) if h == 0 else (lane >= HD)
                none = jnp.zeros_like(q)
                scaled = jnp.where(mine, q * jnp.asarray(HD**-0.5, LOW), none)
                scores = dot_t(k, scaled)
                probs = jnp.exp(scores - lse[0, 0, 2 * pair + h : 2 * pair + h + 1, :])
                grad_probs = dot_t(v, jnp.where(mine, g, none))
                dvs.append(dot(probs.astype(LOW), g))
                inner = jnp.sum(probs * grad_probs, axis=0, keepdims=True)
                grad_scores = (probs * (grad_probs - inner)).astype(LOW)
                dks.append(dot(grad_scores, q))
                dqs.append(dot(k_across[h * HD : (h + 1) * HD], grad_scores))
            scale = HD**-0.5
            dq_low = (jnp.concatenate(dqs, axis=0).T * scale).astype(LOW)
            dk_low = (jnp.where(lane < HD, dks[0], dks[1]) * scale).astype(LOW)
            dv_low = jnp.where(lane < HD, dvs[0], dvs[1]).astype(LOW)
            dq[:, at_cols], dk[:, at_cols], dv[:, at_cols] = dq_low, dk_low, dv_low
            for total, term in ((dq_sum, dq_low), (dv_sum, dv_low)):
                term = jnp.sum(term.astype(jnp.float32), axis=0, keepdims=True)

                @pl.when(pl.program_id(1) == 0)
                def _(total=total, term=term):
                    total[:, at_cols] = term

                @pl.when(pl.program_id(1) > 0)
                def _(total=total, term=term):
                    total[:, at_cols] += term

    block = pl.BlockSpec((length, cols), lambda g, s, at: (s, g))
    total = pl.BlockSpec((1, cols), lambda g, s, at: (0, g))
    table = jax.ShapeDtypeStruct((rows, width), LOW)
    sums = jax.ShapeDtypeStruct((1, width), jnp.float32)
    return kernel_call(
        body,
        (groups, seqs),
        [block] * 4 + [pl.BlockSpec((1, 1, 4, length), lambda g, s, at: (s, g, 0, 0))],
        [block] * 3 + [total] * 2,
        [table] * 3 + [sums] * 2,
        (10 * rows * length * width, 14 * rows * width, rows * length * width // HD),
    )(place.where, query, key, value, grad_context, lse)


def normalised(value):
    centered = value - jnp.mean(value, axis=-1, keepdims=True)
    inverse = lax.rsqrt(jnp.mean(centered * centered, axis=-1, keepdims=True) + 1e-12)
    return centered * inverse, inverse


def normalised_back(grad, unit, inverse, gain):
    inner = grad * gain
    mean = jnp.mean(inner, axis=-1, keepdims=True)
    along = jnp.mean(inner * unit, axis=-1, keepdims=True)
    return (
        inverse * (inner - mean - unit * along),
        jnp.sum(grad * unit, axis=0, keepdims=True),
        jnp.sum(grad, axis=0, keepdims=True),
    )


def feed_in(place, start, context, wo, output_bias, gain, shift, wi, inner_bias):
    rows, width = start.shape
    inner = wi.shape[1]
    tile = width

    def body(at, start, context, wo, ob, gain, shift, wi, ib, unit, inverse, normed_low, active, slope):
        @pl.when(pl.program_id(0) == 0)
        def _():
            first = (
                start[...].astype(jnp.float32)
                + jnp.dot(context[...], wo[...], preferred_element_type=jnp.float32)
                + ob[...]
            )
            u, i = normalised(first)
            unit[...] = u
            inverse[...] = i
            normed_low[...] = (u * gain[...] + shift[...]).astype(LOW)

        for part in range(4):
            cut = slice(part * tile // 4, (part + 1) * tile // 4)
            hidden = (
                jnp.dot(normed_low[...], wi[:, cut], preferred_element_type=jnp.float32) + ib[:, cut]
            )
            below = 0.5 + 0.5 * lax.erf(hidden * 0.7071067811865476)
            active[:, cut] = (hidden * below).astype(LOW)
            bell = jnp.exp(hidden * hidden * -0.5) * 0.3989422804014327
            slope[:, cut] = (below + hidden * bell).astype(LOW)

    keep = lambda a: pl.BlockSpec(a.shape, lambda t, at: (0, 0))
    column = pl.BlockSpec((rows, tile), lambda t, at: (0, t))
    shapes = [
        jax.ShapeDtypeStruct((rows, width), jnp.float32),
        jax.ShapeDtypeStruct((rows, 1), jnp.float32),
        jax.ShapeDtypeStruct((rows, width), LOW),
        jax.ShapeDtypeStruct((rows, inner), LOW),
        jax.ShapeDtypeStruct((rows, inner), LOW),
    ]
    ins = (start, context, wo, output_bias, gain, shift)
    return kernel_call(
        body,
        (inner // tile,),
        [keep(a) for a in ins]
        + [
            pl.BlockSpec((width, tile), lambda t, at: (0, t)),
            pl.BlockSpec((1, tile), lambda t, at: (0, t)),
        ],
        [keep(s) for s in shapes[:3]] + [column, column],
        shapes,
        (2 * rows * width * (width + inner), 2 * width * inner, 2 * rows * inner),
    )(place.where, *ins, wi, inner_bias)


def feed_out(place, active, wu, outer_bias, unit, gain_one, shift_one, gain, shift, cotangent, wanted):
    rows, width = unit.shape
    inner = active.shape[1]
    tile = width
    steps = inner // tile

    def body(at, active, wu, ob, unit, g1, s1, g2, s2, cot, wanted, out, grad, branch, ob_g, g2_g, s2_g, total):
        t = pl.program_id(0)
        term = jnp.dot(active[...], wu[...], preferred_element_type=jnp.float32)

        @pl.when(t == 0)
        def _():
            total[...] = unit[...] * g1[...] + s1[...] + ob[...] + term

        @pl.when(t > 0)
        def _():
            total[...] += term

        @pl.when(t == steps - 1)
        def _():
            u, i = normalised(total[...])
            out[...] = (u * g2[...] + s2[...]).astype(LOW)
            grad_out = cot[...].astype(jnp.float32) * wanted[...]
            back, gain_grad, shift_grad = normalised_back(grad_out, u, i, g2[...])
            grad[...] = back
            low = back.astype(LOW)
            branch[...] = low
            ob_g[...] = jnp.sum(low.astype(jnp.float32), axis=0, keepdims=True)
            g2_g[...] = gain_grad
            s2_g[...] = shift_grad

    keep = lambda a: pl.BlockSpec(a.shape, lambda t, at: (0, 0))
    row = jax.ShapeDtypeStruct((1, width), jnp.float32)
    shapes = [
        jax.ShapeDtypeStruct((rows, width), LOW),
        jax.ShapeDtypeStruct((rows, width), jnp.float32),
        jax.ShapeDtypeStruct((rows, width), LOW),
        row,
        row,
        row,
    ]
    ins = (outer_bias, unit, gain_one, shift_one, gain, shift, cotangent, wanted)
    return kernel_call(
        body,
        (steps,),
        [
            pl.BlockSpec((rows, tile), lambda t, at: (0, t)),
            pl.BlockSpec((tile, width), lambda t, at: (t, 0)),
        ]
        + [keep(a) for a in ins],
        [keep(s) for s in shapes],
        shapes,
        (2 * rows * width * inner, 2 * width * inner, 0),
        [pltpu.VMEM((rows, width), jnp.float32)],
    )(place.where, active, wu, *ins)


def hidden_back(place, grad_branch, wu, slope):
    rows, width = grad_branch.shape
    inner = wu.shape[0]
    tile = width

    def body(at, grad, wu, slope, out, sums):
        back = lax.dot_general(
            grad[...], wu[...], (((1,), (1,)), ((), ())), preferred_element_type=jnp.float32
        )
        low = (back * slope[...].astype(jnp.float32)).astype(LOW)
        out[...] = low
        sums[...] = jnp.sum(low.astype(jnp.float32), axis=0, keepdims=True)

    column = pl.BlockSpec((rows, tile), lambda t, at: (0, t))
    return kernel_call(
        body,
        (inner // tile,),
        [
            pl.BlockSpec((rows, width), lambda t, at: (0, 0)),
            pl.BlockSpec((tile, width), lambda t, at: (t, 0)),
            column,
        ],
        [column, pl.BlockSpec((1, tile), lambda t, at: (0, t))],
        [jax.ShapeDtypeStruct((rows, inner), LOW), jax.ShapeDtypeStruct((1, inner), jnp.float32)],
        (2 * rows * width * inner, 2 * width * inner, 0),
    )(place.where, grad_branch, wu, slope)


def first_back(place, grad_hidden, wi, grad_second, unit, inverse, gain, wo):
    rows, width = grad_second.shape
    inner = wi.shape[1]
    tile = width
    steps = inner // tile

    def body(at, gh, wi, second, unit, inverse, gain, wo, first, low_out, context, ob_g, g_g, s_g, total):
        t = pl.program_id(0)
        term = lax.dot_general(
            gh[...], wi[...], (((1,), (1,)), ((), ())), preferred_element_type=jnp.float32
        )

        @pl.when(t == 0)
        def _():
            total[...] = second[...] + term

        @pl.when(t > 0)
        def _():
            total[...] += term

        @pl.when(t == steps - 1)
        def _():
            back, gain_grad, shift_grad = normalised_back(
                total[...], unit[...], inverse[...], gain[...]
            )
            first[...] = back
            low = back.astype(LOW)
            low_out[...] = low
            ob_g[...] = jnp.sum(low.astype(jnp.float32), axis=0, keepdims=True)
            g_g[...] = gain_grad
            s_g[...] = shift_grad
            context[...] = lax.dot_general(
                low, wo[...], (((1,), (1,)), ((), ())), preferred_element_type=jnp.float32
            ).astype(LOW)

    keep = lambda a: pl.BlockSpec(a.shape, lambda t, at: (0, 0))
    row = jax.ShapeDtypeStruct((1, width), jnp.float32)
    shapes = [
        jax.ShapeDtypeStruct((rows, width), jnp.float32),
        jax.ShapeDtypeStruct((rows, width), LOW),
        jax.ShapeDtypeStruct((rows, width), LOW),
        row,
        row,
        row,
    ]
    ins = (grad_second, unit, inverse, gain, wo)
    return kernel_call(
        body,
        (steps,),
        [
            pl.BlockSpec((rows, tile), lambda t, at: (0, t)),
            pl.BlockSpec((width, tile), lambda t, at: (0, t)),
        ]
        + [keep(a) for a in ins],
        [keep(s) for s in shapes],
        shapes,
        (2 * rows * width * (inner + width), 2 * width * inner, 0),
        [pltpu.VMEM((rows, width), jnp.float32)],
    )(place.where, grad_hidden, wi, *ins)


def start_back(place, grad_first, grads, weights, masked):
    rows, width = grad_first.shape

    def body(at, first, dq, dk, dv, wq, wk, wv, masked, out, sums):
        total = first[...]
        for grad, weight in ((dq, wq), (dk, wk), (dv, wv)):
            total += lax.dot_general(
                grad[...], weight[...], (((1,), (1,)), ((), ())), preferred_element_type=jnp.float32
            )
        hidden = masked[...] > 0.0
        out[...] = jnp.where(hidden, 0.0, total).astype(LOW)
        sums[...] = jnp.sum(jnp.where(hidden, total, 0.0), axis=0, keepdims=True)

    ins = (grad_first, *grads, *weights, masked)
    shapes = [jax.ShapeDtypeStruct((rows, width), LOW), jax.ShapeDtypeStruct((1, width), jnp.float32)]
    return kernel_call(
        body,
        (1,),
        [pl.BlockSpec(a.shape, lambda t, at: (0, 0)) for a in ins],
        [pl.BlockSpec(s.shape, lambda t, at: (0, 0)) for s in shapes],
        shapes,
        (6 * rows * width * width, 6 * width * width, 0),
    )(place.where, *ins)


class PlainGather:
    def __init__(self, rows):
        self.rows = rows

    def step(self, before=(), during=()):
        return None

    def done(self, parts):
        whole = lax.all_gather(self.rows, BOTH, axis=0, tiled=True)
        half = whole.shape[1] // 2
        outs, begin = [], 0
        for width in parts:
            outs.append(
                jnp.concatenate(
                    [whole[:, s * half + begin : s * half + begin + width] for s in range(2)], axis=1
                )
            )
            begin += width
        return outs


class PlainScatter:
    def __init__(self, term):
        self.result = lax.psum_scatter(term, BOTH, scatter_dimension=0, tiled=True)

    def step(self, before=(), during=()):
        return None


class PlainTotal:
    def __init__(self, value):
        self.value = lax.psum(value, BOTH)
        self.strides = [0]

    def step(self, before=(), during=()):
        self.strides.pop(0)


def outer_sum(left, right):
    return jnp.einsum("rd,re->de", left, right, preferred_element_type=jnp.float32)


def halves(place, arrays):
    spots, column = [], 0
    for side in range(2):
        for i, a in enumerate(arrays):
            half = a.shape[1] // 2
            spots.append((i, side * half, half, 0, column))
            column += half
    return pack(place, arrays, spots, (arrays[0].shape[0], column))


def on_device(
    tokens,
    span_starts,
    span_lengths,
    mask_embed,
    query_weight,
    key_weight,
    value_weight,
    output_weight,
    inner_weight,
    outer_weight,
    query_bias,
    value_bias,
    output_bias,
    inner_bias,
    outer_bias,
    gain_one,
    shift_one,
    gain_two,
    shift_two,
    cotangent,
):
    rows, width = tokens.shape
    seqs = span_starts.shape[0]
    length = rows // seqs
    inner = inner_weight.shape[1]
    own_rows, own_tall = query_weight.shape[0], outer_weight.shape[0]
    place = Place()
    staged = own_rows % 8 == 0 and place.chips & (place.chips - 1) == 0
    gather = (lambda piece: Gather(place, piece)) if staged else PlainGather

    first_gather = gather(halves(place, (query_weight, key_weight, value_weight)))
    inner_gather = gather(halves(place, (output_weight, inner_weight)))
    outer_gather = gather(outer_weight)
    first_gather.step()
    places = jnp.arange(length, dtype=jnp.int32)[None, :, None]
    begins = span_starts[:, None, :]
    finish = begins + span_lengths[:, None, :]
    masked = jnp.any((places >= begins) & (places < finish), axis=2)
    edges = jnp.any((places == begins - 1) | (places == finish), axis=2)
    masked = masked.reshape(rows)
    wanted = (masked | edges.reshape(rows)).astype(jnp.float32)[:, None]
    start = jnp.where(masked[:, None], mask_embed[None, :], tokens)
    masked = masked.astype(jnp.float32)[:, None]
    vectors = (
        query_bias,
        value_bias,
        output_bias,
        inner_bias,
        outer_bias,
        gain_one,
        shift_one,
        gain_two,
        shift_two,
    )
    vectors = tuple(v[None] for v in vectors)
    query_row, value_row, output_row, inner_row, outer_row, gain_1, shift_1, gain_2, shift_2 = vectors
    got = first_gather.step(during=(*vectors, start, masked, wanted))
    inner_gather.step((got,))
    got = first_gather.step()
    inner_gather.step((got,))
    got = first_gather.step()
    outer_gather.step((got,))
    inner_gather.step((got,))
    got = first_gather.step()
    weights = first_gather.done((width // 2,) * 3)
    query, key, value, context, lse = attention_forward(
        place, start, weights, query_row, value_row, seqs
    )
    inner_gather.step((got,), (context,))
    outer_gather.step((got,), (context,))
    got = outer_gather.step((context,))
    inner_gather.step((context,))
    wo, wi = inner_gather.done((width // 2, inner // 2))
    unit, inverse, normed_low, active, slope = feed_in(
        place, start, hold(context, got), wo, output_row, gain_1, shift_1, wi, inner_row
    )
    outer_gather.step((), (active,))
    outer_gather.step()
    (wu,) = outer_gather.done((width // 2,))
    layer_output, grad_second, grad_branch, outer_bias_grad, gain_two_grad, shift_two_grad = feed_out(
        place, active, wu, outer_row, unit, gain_1, shift_1, gain_2, shift_2, cotangent, wanted
    )
    if staged:
        outer_sums = Scatter(place, *weight_terms_tall(place, active, grad_branch, own_tall))
        grad_branch = hold(grad_branch, *outer_sums.sends)
    else:
        outer_sums = PlainScatter(outer_sum(active, grad_branch))
    grad_hidden, inner_bias_grad = hidden_back(place, grad_branch, wu, slope)
    got = outer_sums.step((), (grad_hidden,))
    if staged:
        tiles = inner // width
        inner_sums = Scatter(
            place, *weight_terms(place, [normed_low] * tiles, hold(grad_hidden, got), own_rows)
        )
        grad_hidden = hold(grad_hidden, *inner_sums.sends)
    else:
        inner_sums = PlainScatter(outer_sum(normed_low, grad_hidden))
    grad_first, grad_attended, grad_context, output_bias_grad, gain_one_grad, shift_one_grad = first_back(
        place, grad_hidden, wi, grad_second, unit, inverse, gain_1, wo
    )
    got = outer_sums.step((), (grad_context,))
    grad_query, grad_key, grad_value, query_bias_grad, value_bias_grad = attention_backward(
        place, query, key, value, hold(grad_context, got), lse
    )
    got = outer_sums.step((), (grad_query,))
    inner_sums.step((grad_context,), (grad_query,))
    lefts = [start, start, start, context]
    rights = [hold(grad_query, got), grad_key, grad_value, grad_attended]
    if staged:
        first_sums = Scatter(place, *weight_terms(place, lefts, rights, own_rows))
        grad_query = hold(grad_query, *first_sums.sends)
    else:
        first_sums = PlainScatter(
            jnp.concatenate([outer_sum(l, r) for l, r in zip(lefts, rights)], axis=1)
        )
    input_grad, mask_grad = start_back(
        place, grad_first, (grad_query, grad_key, grad_value), weights, masked
    )
    got_outer = outer_sums.step((), (mask_grad,))
    got = inner_sums.step((), (mask_grad,))
    first_sums.step((), (mask_grad,))
    smalls = (
        query_bias_grad,
        value_bias_grad,
        output_bias_grad,
        outer_bias_grad,
        gain_one_grad,
        shift_one_grad,
        gain_two_grad,
        shift_two_grad,
        mask_grad,
        inner_bias_grad,
    )
    spots = [(i, 0, width, i, 0) for i in range(9)]
    spots += [(9, i * width, width, 9 + i, 0) for i in range(inner // width)]
    high = -(-(9 + inner // width) // 8) * 8
    packed = pack(place, smalls, spots, (high, width))
    total = Total(place, packed) if staged else PlainTotal(packed)
    got = inner_sums.step((got,))
    got = first_sums.step((got_outer,))
    outer_sums.step((got_outer,))
    if staged:
        total.step((got_outer,))
        inner_sums.step((got,))
        got = first_sums.step((got,))
        total.step()
        got = first_sums.step()
        inner_sums.step((got,))
        total.step()
        got = first_sums.step()
        total.step()
        total.step()
    else:
        total.step()
    packed = total.value
    order = (0, 1, 2, 9, 3, 4, 5, 6, 7, 8)
    firsts = first_sums.result
    return (
        layer_output,
        input_grad,
        *(firsts[:, i * width : (i + 1) * width] for i in range(4)),
        inner_sums.result,
        outer_sums.result,
        *(packed[9:9 + inner // width].reshape(-1) if i == 9 else packed[i] for i in order),
    )


def solution(mesh):
    placed = (
        P(("dp", "pair"), None),
        P(("dp", "pair"), None),
        P(("dp", "pair"), None),
        P(),
        P(("dp", "pair"), None),
        P(("dp", "pair"), None),
        P(("dp", "pair"), None),
        P(("dp", "pair"), None),
        P(("dp", "pair"), None),
        P(("dp", "pair"), None),
        P(),
        P(),
        P(),
        P(),
        P(),
        P(),
        P(),
        P(),
        P(),
        P(("dp", "pair"), None),
    )
    return jax.shard_map(
        on_device,
        mesh=mesh,
        in_specs=placed,
        out_specs=(
            P(("dp", "pair"), None),
            P(("dp", "pair"), None),
            P(("dp", "pair"), None),
            P(("dp", "pair"), None),
            P(("dp", "pair"), None),
            P(("dp", "pair"), None),
            P(("dp", "pair"), None),
            P(("dp", "pair"), None),
            P(),
            P(),
            P(),
            P(),
            P(),
            P(),
            P(),
            P(),
            P(),
            P(),
        ),
        check_vma=False,
    )
```

```python
import jax
import jax.numpy as jnp
from jax import lax
from jax.experimental import pallas as pl
from jax.experimental.pallas import tpu as pltpu
from jax.sharding import PartitionSpec as P

HD = 64
BOTH = ("dp", "pair")
LOW = jnp.bfloat16
COVER = 30


def hold(value, *others):
    others = [o for o in others if o is not None]
    return lax.optimization_barrier((value, *others))[0] if others else value


class Place:
    def __init__(self):
        self.chips = lax.axis_size("dp")
        fast = 1
        while (2 * fast) ** 3 <= self.chips:
            fast *= 2
        strides = []
        while (1 << len(strides)) < self.chips:
            strides.insert(0, self.chips >> (len(strides) + 1))
        strides = sorted(strides, reverse=True)
        self.fast = [b for b in strides if b < fast]
        self.mid = [b for b in strides if fast <= b < fast * fast]
        self.slow = [b for b in strides if b >= fast * fast]
        self.chip = lax.axis_index("dp")
        self.core = lax.axis_index("pair")
        self.where = jnp.stack([self.chip, self.core]).astype(jnp.int32)

    def swap(self, value, stride):
        return lax.ppermute(value, "dp", [(i, i ^ stride) for i in range(self.chips)])

    def swap_core(self, value):
        return lax.ppermute(value, "pair", [(0, 1), (1, 0)])


def kernel_call(body, grid, in_specs, out_specs, out_shape, cost, scratch=(), limit=None):
    flops, moved, special = cost
    return pl.pallas_call(
        body,
        grid_spec=pltpu.PrefetchScalarGridSpec(
            num_scalar_prefetch=1,
            grid=grid,
            in_specs=in_specs,
            out_specs=out_specs,
            scratch_shapes=scratch,
        ),
        out_shape=out_shape,
        cost_estimate=pl.CostEstimate(
            flops=COVER * flops, bytes_accessed=moved if flops == 0 else COVER * moved, transcendentals=special
        ),
        compiler_params=pltpu.CompilerParams(vmem_limit_bytes=limit or 16 * 2**20),
    )


def pack(place, arrays, spots, shape):
    def body(at, *refs):
        out = refs[-1]
        for i, begin, width, row, column in spots:
            value = refs[i][:, begin : begin + width]
            out[row : row + value.shape[0], column : column + width] = value

    moved = 2 * sum(a.size * a.dtype.itemsize for a in arrays)
    return kernel_call(
        body,
        (1,),
        [pl.BlockSpec(a.shape, lambda i, at: (0, 0)) for a in arrays],
        pl.BlockSpec(shape, lambda i, at: (0, 0)),
        jax.ShapeDtypeStruct(shape, arrays[0].dtype),
        (0, moved, 0),
    )(place.where, *arrays)


class Gather:
    def __init__(self, place, rows):
        self.place = place
        self.slots = rows[None]
        self.left = place.slow + place.mid + place.fast
        self.right = place.slow + place.fast + place.mid
        self.stage = 0
        self.halves = None
        self.ready = ()

    def step(self, before=(), during=()):
        place, stage = self.place, self.stage
        self.stage += 1
        if stage < len(place.slow):
            value = hold(self.slots, *before)
            got = hold(place.swap(value, self.left[stage]), *during)
            self.slots = jnp.concatenate([value, got])
            self.ready = (self.slots,)
            if self.stage == len(place.slow):
                half = self.slots.shape[-1] // 2
                self.halves = self.ready = (self.slots[..., :half], self.slots[..., half:])
            return got
        if stage < len(self.left):
            l, r = (hold(v, *before) for v in self.halves)
            gl = hold(place.swap(l, self.left[stage]), *during)
            gr = hold(place.swap(r, self.right[stage]), *during)
            self.halves = self.ready = (jnp.concatenate([l, gl]), jnp.concatenate([r, gr]))
            if self.stage == len(self.left):
                self.stacked = jnp.stack(self.halves)
                self.ready = (self.stacked,)
            return gr
        self.own = hold(self.stacked, *before)
        self.other = hold(place.swap_core(self.own), *during)
        return self.other

    def done(self, parts):
        place = self.place
        _, chips, rows, half = self.own.shape
        orders = (self.left, self.right)

        def body(at, own, other, *outs):
            chip, core = at[0], at[1]
            for side in range(2):

                def put(j, carry):
                    to = chip
                    for i, stride in enumerate(orders[side]):
                        to = to ^ (((j >> i) & 1) * stride)
                    begin = 0
                    for out, width in zip(outs, parts):
                        cols = slice(side * width, (side + 1) * width)
                        out[2 * to + core, :, cols] = own[side, j, :, begin : begin + width]
                        out[2 * to + 1 - core, :, cols] = other[side, j, :, begin : begin + width]
                        begin += width
                    return carry

                lax.fori_loop(0, chips, put, 0)

        moved = 8 * chips * rows * half * 2
        whole = pl.BlockSpec((2, chips, rows, half), lambda i, at: (0, 0, 0, 0))
        outs = kernel_call(
            body,
            (1,),
            [whole, whole],
            [pl.BlockSpec((2 * chips, rows, 2 * w), lambda i, at: (0, 0, 0)) for w in parts],
            [jax.ShapeDtypeStruct((2 * chips, rows, 2 * w), LOW) for w in parts],
            (0, moved, 0),
        )(place.where, self.own, self.other)
        return [o.reshape(-1, o.shape[-1]) for o in outs]


def fold(place, keeps, gots, bits, join):
    sides = len(bits)
    deep = keeps[0].ndim == 4
    chips, rows, cols = keeps[0].shape[-3:]
    steps = next(s for s in (3, 2, 1) if rows % (8 * s) == 0)
    part = rows // steps

    def body(at, *refs):
        ins, outs = refs[: 2 * len(keeps)], refs[2 * len(keeps) :]
        for side in range(sides):
            for j in range(chips):
                if deep:
                    a, b = ins[0][side, j], ins[1][side, j]
                else:
                    a, b = ins[side][j], ins[len(keeps) + side][j]
                total = (a.astype(jnp.float32) + b.astype(jnp.float32)).astype(LOW)
                low = bits[side]
                to = (j // (2 * low)) * low + j % low
                goes = (j // low) % 2
                if join:
                    outs[goes][to, :, side * cols : (side + 1) * cols] = total
                else:
                    outs[goes * sides + side][to] = total

    if deep:
        ins = pl.BlockSpec((2, chips, part, cols), lambda i, at: (0, 0, i, 0))
    else:
        ins = pl.BlockSpec((chips, part, cols), lambda i, at: (0, i, 0))
    wide = cols * sides if join else cols
    count = 2 if join else 2 * sides
    outs = kernel_call(
        body,
        (steps,),
        [ins] * (2 * len(keeps)),
        [pl.BlockSpec((chips // 2, part, wide), lambda i, at: (0, i, 0))] * count,
        [jax.ShapeDtypeStruct((chips // 2, rows, wide), LOW)] * count,
        (0, 6 * sides * chips * rows * cols, 0),
    )(place.where, *keeps, *gots)
    return list(outs[: count // 2]), list(outs[count // 2 :])


class Scatter:
    def __init__(self, place, keep, send):
        self.place = place
        self.keeps, self.sends = [keep], [send]
        self.left = (place.slow + place.mid + place.fast)[::-1]
        self.right = (place.slow + place.fast + place.mid)[::-1]
        self.held = [sorted(self.left), sorted(self.right)]
        self.stage = -1
        self.result = None
        self.gots = None

    def fold(self):
        place = self.place
        if self.gots is not None:
            orders = (self.left, self.right)
            crossing = len(self.left) - len(place.slow)
            sides = 2 if self.stage <= crossing else 1
            bits = []
            for side in range(sides):
                stride = orders[side][self.stage]
                bits.append(1 << self.held[side].index(stride))
                self.held[side].remove(stride)
            join = self.stage == crossing
            self.keeps, self.sends = fold(place, self.keeps, self.gots, bits, join)
        return self.sends

    def send(self, before=(), during=()):
        place = self.place
        swaps = (
            [place.swap_core]
            if self.stage < 0
            else [lambda v, b=o[self.stage]: place.swap(v, b) for o in (self.left, self.right)]
        )
        self.gots = [
            hold(swap(hold(v, *before)), *during) for v, swap in zip(self.sends, swaps)
        ]
        self.stage += 1
        if self.stage == len(self.left):
            self.result = self.keeps[0][0].astype(jnp.float32) + self.gots[0][0].astype(jnp.float32)
        return self.gots


def weight_terms(place, lefts, rights, rows):
    chips = place.chips
    count = len(lefts)
    length, features = lefts[0].shape
    joined = not isinstance(rights, list)
    width = rights.shape[1] // count if joined else rights[0].shape[1]
    per = count // 2
    unique = []
    for l in lefts:
        if not any(l is u for u in unique):
            unique.append(l)
    which = [next(i for i, u in enumerate(unique) if u is l) for l in lefts]
    rights = [rights] if joined else rights

    def body(at, *refs):
        ins, (keep, send) = refs[:-2], refs[-2:]
        t = pl.program_id(0)
        chip, core = at[0], at[1]

        def one(left, right):
            total = lax.dot_general(
                left[...], right[...], (((0,), (0,)), ((), ())), preferred_element_type=jnp.float32
            )
            for c in range(chips):
                to = c ^ chip
                a = total[2 * c * rows : (2 * c + 1) * rows].astype(LOW)
                b = total[(2 * c + 1) * rows : (2 * c + 2) * rows].astype(LOW)
                keep[0, to] = jnp.where(core == 0, a, b)
                send[0, to] = jnp.where(core == 0, b, a)

        if joined:
            one(ins[0], ins[1])
        else:
            for k in range(count):
                pl.when(t == k)(lambda k=k: one(ins[which[k]], ins[len(unique) + k]))

    block = pl.BlockSpec((1, chips, rows, width), lambda t, at: (t // per, 0, 0, t % per))
    shape = jax.ShapeDtypeStruct((2, chips, rows, width * per), LOW)
    fixed = pl.BlockSpec((length, width), lambda t, at: (0, 0))
    return kernel_call(
        body,
        (count,),
        [pl.BlockSpec((length, features), lambda t, at: (0, 0)) for _ in unique]
        + ([pl.BlockSpec((length, width), lambda t, at: (0, t))] if joined else [fixed] * count),
        [block, block],
        [shape, shape],
        (2 * count * length * features * width, 4 * count * features * width, 0),
    )(place.where, *unique, *rights)


def weight_terms_tall(place, left, right, rows):
    chips = place.chips
    length, features = left.shape
    width = right.shape[1]
    tiles = 4
    group = chips // tiles

    def body(at, left_ref, right_ref, keep, send):
        chip, core = at[0], at[1]
        total = lax.dot_general(
            left_ref[...], right_ref[...], (((0,), (0,)), ((), ())), preferred_element_type=jnp.float32
        )
        for c in range(group):
            to = c ^ (chip % group)
            a = total[2 * c * rows : (2 * c + 1) * rows].astype(LOW)
            b = total[(2 * c + 1) * rows : (2 * c + 2) * rows].astype(LOW)
            own, other = jnp.where(core == 0, a, b), jnp.where(core == 0, b, a)
            for side in range(2):
                cols = slice(side * (width // 2), (side + 1) * (width // 2))
                keep[side, to] = own[:, cols]
                send[side, to] = other[:, cols]

    block = pl.BlockSpec((2, group, rows, width // 2), lambda t, at: (0, t, 0, 0))
    shape = jax.ShapeDtypeStruct((2, chips, rows, width // 2), LOW)
    return kernel_call(
        body,
        (tiles,),
        [
            pl.BlockSpec((length, features // tiles), lambda t, at: (0, t ^ (at[0] // group))),
            pl.BlockSpec((length, width), lambda t, at: (0, 0)),
        ],
        [block, block],
        [shape, shape],
        (2 * length * features * width, 4 * features * width, 0),
    )(place.where, left, right)


class Total:
    def __init__(self, place, value):
        self.place, self.value = place, value
        self.strides = [0] + place.fast + place.mid + place.slow

    def step(self, before=(), during=()):
        if not self.strides:
            return None
        value = hold(self.value, *before)
        stride = self.strides.pop(0)
        got = hold(self.place.swap(value, stride) if stride else self.place.swap_core(value), *during)
        self.value = value + got
        return got


def attention_forward(place, start, weights, query_bias, value_bias, seqs):
    rows, width = start.shape
    length = rows // seqs
    cols = 4 * HD
    groups = width // cols

    def body(at, start, wq, wk, wv, qb, vb, query, key, value, context, lse):
        x = start[...]
        dot = lambda l, r: jnp.dot(l, r, preferred_element_type=jnp.float32)
        query[...] = (dot(x, wq[...]) + qb[...]).astype(LOW)
        key[...] = dot(x, wk[...]).astype(LOW)
        value[...] = (dot(x, wv[...]) + vb[...]).astype(LOW)
        lane = lax.broadcasted_iota(jnp.int32, (length, 2 * HD), 1)
        for pair in range(2):
            at_cols = slice(pair * 2 * HD, (pair + 1) * 2 * HD)
            q, k = query[:, at_cols], key[:, at_cols]
            v_across = value[:, at_cols].T
            mixed = []
            for h in range(2):
                mine = (lane < HD) if h == 0 else (lane >= HD)
                q_mine = jnp.where(mine, q * jnp.asarray(HD**-0.5, LOW), jnp.zeros_like(q))
                scores = lax.dot_general(
                    k, q_mine, (((1,), (1,)), ((), ())), preferred_element_type=jnp.float32
                )
                most = jnp.max(scores, axis=0, keepdims=True)
                raised = jnp.exp(scores - most)
                total = jnp.sum(raised, axis=0, keepdims=True)
                probs = (raised * (1.0 / total)).astype(LOW)
                mixed.append(dot(v_across[h * HD : (h + 1) * HD], probs))
                lse[0, 0, 2 * pair + h : 2 * pair + h + 1, :] = most + jnp.log(total)
            context[:, at_cols] = jnp.concatenate(mixed, axis=0).T.astype(LOW)

    block = pl.BlockSpec((length, cols), lambda s, g, at: (s, g))
    weight = pl.BlockSpec((width, cols), lambda s, g, at: (0, g))
    bias = pl.BlockSpec((1, cols), lambda s, g, at: (0, g))
    table = jax.ShapeDtypeStruct((rows, width), LOW)
    return kernel_call(
        body,
        (seqs, groups),
        [pl.BlockSpec((length, width), lambda s, g, at: (s, 0)), weight, weight, weight, bias, bias],
        [block] * 4 + [pl.BlockSpec((1, 1, 4, length), lambda s, g, at: (s, g, 0, 0))],
        [table] * 4 + [jax.ShapeDtypeStruct((seqs, groups, 4, length), jnp.float32)],
        (6 * rows * width * width, 6 * width * width, seqs * groups * 4 * length * length),
    )(place.where, start, *weights, query_bias, value_bias)


def attention_backward(place, query, key, value, grad_context, lse):
    rows, width = query.shape
    seqs, groups, _, length = lse.shape
    cols = 4 * HD

    def body(at, query, key, value, grad, lse, dq, dk, dv, dq_sum, dv_sum):
        dot = lambda l, r: jnp.dot(l, r, preferred_element_type=jnp.float32)
        dot_t = lambda l, r: lax.dot_general(
            l, r, (((1,), (1,)), ((), ())), preferred_element_type=jnp.float32
        )
        lane = lax.broadcasted_iota(jnp.int32, (length, 2 * HD), 1)
        for pair in range(2):
            at_cols = slice(pair * 2 * HD, (pair + 1) * 2 * HD)
            q, k, v, g = query[:, at_cols], key[:, at_cols], value[:, at_cols], grad[:, at_cols]
            k_across = k.T
            dqs, dks, dvs = [], [], []
            for h in range(2):
                mine = (lane < HD) if h == 0 else (lane >= HD)
                none = jnp.zeros_like(q)
                scaled = jnp.where(mine, q * jnp.asarray(HD**-0.5, LOW), none)
                scores = dot_t(k, scaled)
                probs = jnp.exp(scores - lse[0, 0, 2 * pair + h : 2 * pair + h + 1, :])
                grad_probs = dot_t(v, jnp.where(mine, g, none))
                dvs.append(dot(probs.astype(LOW), g))
                inner = jnp.sum(probs * grad_probs, axis=0, keepdims=True)
                grad_scores = (probs * (grad_probs - inner)).astype(LOW)
                dks.append(dot(grad_scores, q))
                dqs.append(dot(k_across[h * HD : (h + 1) * HD], grad_scores))
            scale = HD**-0.5
            dq_low = (jnp.concatenate(dqs, axis=0).T * scale).astype(LOW)
            dk_low = (jnp.where(lane < HD, dks[0], dks[1]) * scale).astype(LOW)
            dv_low = jnp.where(lane < HD, dvs[0], dvs[1]).astype(LOW)
            dq[:, at_cols], dk[:, at_cols], dv[:, at_cols] = dq_low, dk_low, dv_low
            for total, term in ((dq_sum, dq_low), (dv_sum, dv_low)):
                term = jnp.sum(term.astype(jnp.float32), axis=0, keepdims=True)

                @pl.when(pl.program_id(1) == 0)
                def _(total=total, term=term):
                    total[:, at_cols] = term

                @pl.when(pl.program_id(1) > 0)
                def _(total=total, term=term):
                    total[:, at_cols] += term

    block = pl.BlockSpec((length, cols), lambda g, s, at: (s, g))
    total = pl.BlockSpec((1, cols), lambda g, s, at: (0, g))
    table = jax.ShapeDtypeStruct((rows, width), LOW)
    sums = jax.ShapeDtypeStruct((1, width), jnp.float32)
    return kernel_call(
        body,
        (groups, seqs),
        [block] * 4 + [pl.BlockSpec((1, 1, 4, length), lambda g, s, at: (s, g, 0, 0))],
        [block] * 3 + [total] * 2,
        [table] * 3 + [sums] * 2,
        (10 * rows * length * width, 14 * rows * width, rows * length * width // HD),
    )(place.where, query, key, value, grad_context, lse)


def normalised(value):
    centered = value - jnp.mean(value, axis=-1, keepdims=True)
    inverse = lax.rsqrt(jnp.mean(centered * centered, axis=-1, keepdims=True) + 1e-12)
    return centered * inverse, inverse


def normalised_back(grad, unit, inverse, gain):
    inner = grad * gain
    mean = jnp.mean(inner, axis=-1, keepdims=True)
    along = jnp.mean(inner * unit, axis=-1, keepdims=True)
    return (
        inverse * (inner - mean - unit * along),
        jnp.sum(grad * unit, axis=0, keepdims=True),
        jnp.sum(grad, axis=0, keepdims=True),
    )


def feed_in(place, start, context, wo, output_bias, gain, shift, wi, inner_bias):
    rows, width = start.shape
    inner = wi.shape[1]
    tile = width

    def body(at, start, context, wo, ob, gain, shift, wi, ib, unit, inverse, normed_low, active, slope):
        @pl.when(pl.program_id(0) == 0)
        def _():
            first = (
                start[...].astype(jnp.float32)
                + jnp.dot(context[...], wo[...], preferred_element_type=jnp.float32)
                + ob[...]
            )
            u, i = normalised(first)
            unit[...] = u
            inverse[...] = i
            normed_low[...] = (u * gain[...] + shift[...]).astype(LOW)

        for part in range(4):
            cut = slice(part * tile // 4, (part + 1) * tile // 4)
            hidden = (
                jnp.dot(normed_low[...], wi[:, cut], preferred_element_type=jnp.float32) + ib[:, cut]
            )
            below = 0.5 + 0.5 * lax.erf(hidden * 0.7071067811865476)
            active[:, cut] = (hidden * below).astype(LOW)
            bell = jnp.exp(hidden * hidden * -0.5) * 0.3989422804014327
            slope[:, cut] = (below + hidden * bell).astype(LOW)

    keep = lambda a: pl.BlockSpec(a.shape, lambda t, at: (0, 0))
    column = pl.BlockSpec((rows, tile), lambda t, at: (0, t))
    shapes = [
        jax.ShapeDtypeStruct((rows, width), jnp.float32),
        jax.ShapeDtypeStruct((rows, 1), jnp.float32),
        jax.ShapeDtypeStruct((rows, width), LOW),
        jax.ShapeDtypeStruct((rows, inner), LOW),
        jax.ShapeDtypeStruct((rows, inner), LOW),
    ]
    ins = (start, context, wo, output_bias, gain, shift)
    return kernel_call(
        body,
        (inner // tile,),
        [keep(a) for a in ins]
        + [
            pl.BlockSpec((width, tile), lambda t, at: (0, t)),
            pl.BlockSpec((1, tile), lambda t, at: (0, t)),
        ],
        [keep(s) for s in shapes[:3]] + [column, column],
        shapes,
        (2 * rows * width * (width + inner), 2 * width * inner, 2 * rows * inner),
    )(place.where, *ins, wi, inner_bias)


def feed_out(place, active, wu, outer_bias, unit, gain_one, shift_one, gain, shift, cotangent, wanted):
    rows, width = unit.shape
    inner = active.shape[1]
    tile = width
    steps = inner // tile

    def body(at, active, wu, ob, unit, g1, s1, g2, s2, cot, wanted, out, grad, branch, ob_g, g2_g, s2_g, total):
        t = pl.program_id(0)
        term = jnp.dot(active[...], wu[...], preferred_element_type=jnp.float32)

        @pl.when(t == 0)
        def _():
            total[...] = unit[...] * g1[...] + s1[...] + ob[...] + term

        @pl.when(t > 0)
        def _():
            total[...] += term

        @pl.when(t == steps - 1)
        def _():
            u, i = normalised(total[...])
            out[...] = (u * g2[...] + s2[...]).astype(LOW)
            grad_out = cot[...].astype(jnp.float32) * wanted[...]
            back, gain_grad, shift_grad = normalised_back(grad_out, u, i, g2[...])
            grad[...] = back
            low = back.astype(LOW)
            branch[...] = low
            ob_g[...] = jnp.sum(low.astype(jnp.float32), axis=0, keepdims=True)
            g2_g[...] = gain_grad
            s2_g[...] = shift_grad

    keep = lambda a: pl.BlockSpec(a.shape, lambda t, at: (0, 0))
    row = jax.ShapeDtypeStruct((1, width), jnp.float32)
    shapes = [
        jax.ShapeDtypeStruct((rows, width), LOW),
        jax.ShapeDtypeStruct((rows, width), jnp.float32),
        jax.ShapeDtypeStruct((rows, width), LOW),
        row,
        row,
        row,
    ]
    ins = (outer_bias, unit, gain_one, shift_one, gain, shift, cotangent, wanted)
    return kernel_call(
        body,
        (steps,),
        [
            pl.BlockSpec((rows, tile), lambda t, at: (0, t)),
            pl.BlockSpec((tile, width), lambda t, at: (t, 0)),
        ]
        + [keep(a) for a in ins],
        [keep(s) for s in shapes],
        shapes,
        (2 * rows * width * inner, 2 * width * inner, 0),
        [pltpu.VMEM((rows, width), jnp.float32)],
    )(place.where, active, wu, *ins)


def hidden_back(place, grad_branch, wu, slope):
    rows, width = grad_branch.shape
    inner = wu.shape[0]
    tile = width

    def body(at, grad, wu, slope, out, sums):
        back = lax.dot_general(
            grad[...], wu[...], (((1,), (1,)), ((), ())), preferred_element_type=jnp.float32
        )
        low = (back * slope[...].astype(jnp.float32)).astype(LOW)
        out[...] = low
        sums[...] = jnp.sum(low.astype(jnp.float32), axis=0, keepdims=True)

    column = pl.BlockSpec((rows, tile), lambda t, at: (0, t))
    return kernel_call(
        body,
        (inner // tile,),
        [
            pl.BlockSpec((rows, width), lambda t, at: (0, 0)),
            pl.BlockSpec((tile, width), lambda t, at: (t, 0)),
            column,
        ],
        [column, pl.BlockSpec((1, tile), lambda t, at: (0, t))],
        [jax.ShapeDtypeStruct((rows, inner), LOW), jax.ShapeDtypeStruct((1, inner), jnp.float32)],
        (2 * rows * width * inner, 2 * width * inner, 0),
    )(place.where, grad_branch, wu, slope)


def first_back(place, grad_hidden, wi, grad_second, unit, inverse, gain, wo):
    rows, width = grad_second.shape
    inner = wi.shape[1]
    tile = width
    steps = inner // tile

    def body(at, gh, wi, second, unit, inverse, gain, wo, first, low_out, context, ob_g, g_g, s_g, total):
        t = pl.program_id(0)
        term = lax.dot_general(
            gh[...], wi[...], (((1,), (1,)), ((), ())), preferred_element_type=jnp.float32
        )

        @pl.when(t == 0)
        def _():
            total[...] = second[...] + term

        @pl.when(t > 0)
        def _():
            total[...] += term

        @pl.when(t == steps - 1)
        def _():
            back, gain_grad, shift_grad = normalised_back(
                total[...], unit[...], inverse[...], gain[...]
            )
            first[...] = back
            low = back.astype(LOW)
            low_out[...] = low
            ob_g[...] = jnp.sum(low.astype(jnp.float32), axis=0, keepdims=True)
            g_g[...] = gain_grad
            s_g[...] = shift_grad
            context[...] = lax.dot_general(
                low, wo[...], (((1,), (1,)), ((), ())), preferred_element_type=jnp.float32
            ).astype(LOW)

    keep = lambda a: pl.BlockSpec(a.shape, lambda t, at: (0, 0))
    row = jax.ShapeDtypeStruct((1, width), jnp.float32)
    shapes = [
        jax.ShapeDtypeStruct((rows, width), jnp.float32),
        jax.ShapeDtypeStruct((rows, width), LOW),
        jax.ShapeDtypeStruct((rows, width), LOW),
        row,
        row,
        row,
    ]
    ins = (grad_second, unit, inverse, gain, wo)
    return kernel_call(
        body,
        (steps,),
        [
            pl.BlockSpec((rows, tile), lambda t, at: (0, t)),
            pl.BlockSpec((width, tile), lambda t, at: (0, t)),
        ]
        + [keep(a) for a in ins],
        [keep(s) for s in shapes],
        shapes,
        (2 * rows * width * (inner + width), 2 * width * inner, 0),
        [pltpu.VMEM((rows, width), jnp.float32)],
    )(place.where, grad_hidden, wi, *ins)


def start_back(place, grad_first, grads, weights, masked):
    rows, width = grad_first.shape

    def body(at, first, dq, dk, dv, wq, wk, wv, masked, out, sums):
        total = first[...]
        for grad, weight in ((dq, wq), (dk, wk), (dv, wv)):
            total += lax.dot_general(
                grad[...], weight[...], (((1,), (1,)), ((), ())), preferred_element_type=jnp.float32
            )
        hidden = masked[...] > 0.0
        out[...] = jnp.where(hidden, 0.0, total).astype(LOW)
        sums[...] = jnp.sum(jnp.where(hidden, total, 0.0), axis=0, keepdims=True)

    ins = (grad_first, *grads, *weights, masked)
    shapes = [jax.ShapeDtypeStruct((rows, width), LOW), jax.ShapeDtypeStruct((1, width), jnp.float32)]
    return kernel_call(
        body,
        (1,),
        [pl.BlockSpec(a.shape, lambda t, at: (0, 0)) for a in ins],
        [pl.BlockSpec(s.shape, lambda t, at: (0, 0)) for s in shapes],
        shapes,
        (6 * rows * width * width, 6 * width * width, 0),
    )(place.where, *ins)


class PlainGather:
    def __init__(self, rows):
        self.rows = rows
        self.ready = ()

    def step(self, before=(), during=()):
        return None

    def done(self, parts):
        whole = lax.all_gather(self.rows, BOTH, axis=0, tiled=True)
        half = whole.shape[1] // 2
        outs, begin = [], 0
        for width in parts:
            outs.append(
                jnp.concatenate(
                    [whole[:, s * half + begin : s * half + begin + width] for s in range(2)], axis=1
                )
            )
            begin += width
        return outs


class PlainScatter:
    def __init__(self, term):
        self.result = lax.psum_scatter(term, BOTH, scatter_dimension=0, tiled=True)
        self.sends = ()

    def fold(self):
        return ()

    def send(self, before=(), during=()):
        return ()


class PlainTotal:
    def __init__(self, value):
        self.value = lax.psum(value, BOTH)

    def step(self, before=(), during=()):
        return None


def outer_sum(left, right):
    return jnp.einsum("rd,re->de", left, right, preferred_element_type=jnp.float32)


def halves(place, arrays):
    spots, column = [], 0
    for side in range(2):
        for i, a in enumerate(arrays):
            half = a.shape[1] // 2
            spots.append((i, side * half, half, 0, column))
            column += half
    return pack(place, arrays, spots, (arrays[0].shape[0], column))


def on_device(
    tokens,
    span_starts,
    span_lengths,
    mask_embed,
    query_weight,
    key_weight,
    value_weight,
    output_weight,
    inner_weight,
    outer_weight,
    query_bias,
    value_bias,
    output_bias,
    inner_bias,
    outer_bias,
    gain_one,
    shift_one,
    gain_two,
    shift_two,
    cotangent,
):
    rows, width = tokens.shape
    seqs = span_starts.shape[0]
    length = rows // seqs
    inner = inner_weight.shape[1]
    own_rows, own_tall = query_weight.shape[0], outer_weight.shape[0]
    place = Place()
    staged = own_rows % 8 == 0 and place.chips & (place.chips - 1) == 0
    gather = (lambda piece: Gather(place, piece)) if staged else PlainGather

    first_gather = gather(halves(place, (query_weight, key_weight, value_weight)))
    inner_gather = gather(halves(place, (output_weight, inner_weight)))
    outer_gather = gather(outer_weight)
    first_gather.step()
    places = jnp.arange(length, dtype=jnp.int32)[None, :, None]
    begins = span_starts[:, None, :]
    finish = begins + span_lengths[:, None, :]
    masked = jnp.any((places >= begins) & (places < finish), axis=2)
    edges = jnp.any((places == begins - 1) | (places == finish), axis=2)
    masked = masked.reshape(rows)
    wanted = (masked | edges.reshape(rows)).astype(jnp.float32)[:, None]
    start = jnp.where(masked[:, None], mask_embed[None, :], tokens)
    masked = masked.astype(jnp.float32)[:, None]
    vectors = (
        query_bias,
        value_bias,
        output_bias,
        inner_bias,
        outer_bias,
        gain_one,
        shift_one,
        gain_two,
        shift_two,
    )
    vectors = tuple(v[None] for v in vectors)
    query_row, value_row, output_row, inner_row, outer_row, gain_1, shift_1, gain_2, shift_2 = vectors
    first_gather.step(during=(*vectors, start, masked, wanted))
    before = first_gather.ready
    first_gather.step()
    inner_gather.step(before, first_gather.ready)
    before = first_gather.ready
    first_gather.step()
    inner_gather.step(before, first_gather.ready)
    outer_gather.step(inner_gather.ready)
    inner_gather.step(first_gather.ready)
    got = first_gather.step()
    weights = first_gather.done((width // 2,) * 3)
    query, key, value, context, lse = attention_forward(
        place, hold(start, *inner_gather.ready, *outer_gather.ready), weights, query_row, value_row, seqs
    )
    outer_gather.step(inner_gather.ready, (context,))
    inner_gather.step((got,), (context, *outer_gather.ready))
    got = inner_gather.step((context,))
    outer_gather.step(inner_gather.ready, (got,))
    wo, wi = inner_gather.done((width // 2, inner // 2))
    unit, inverse, normed_low, active, slope = feed_in(
        place, start, hold(context, *outer_gather.ready), wo, output_row, gain_1, shift_1, wi, inner_row
    )
    outer_gather.step((), (active,))
    outer_gather.step()
    (wu,) = outer_gather.done((width // 2,))
    layer_output, grad_second, grad_branch, outer_bias_grad, gain_two_grad, shift_two_grad = feed_out(
        place, active, wu, outer_row, unit, gain_1, shift_1, gain_2, shift_2, cotangent, wanted
    )
    if staged:
        outer_sums = Scatter(place, *weight_terms_tall(place, active, grad_branch, own_tall))
    else:
        outer_sums = PlainScatter(outer_sum(active, grad_branch))
    grad_hidden, inner_bias_grad = hidden_back(place, hold(grad_branch, *outer_sums.sends), wu, slope)
    outer_sums.send((), (grad_hidden,))
    outer_sums.fold()
    if staged:
        tiles = inner // width
        grad_tied = hold(grad_hidden, *outer_sums.sends)
        inner_sums = Scatter(place, *weight_terms(place, [normed_low] * tiles, grad_tied, own_rows))
    else:
        inner_sums = PlainScatter(outer_sum(normed_low, grad_hidden))
    outer_sums.send((), inner_sums.sends)
    outer_sums.fold()
    tied = hold(grad_hidden, *inner_sums.sends, *outer_sums.sends)
    grad_first, grad_attended, grad_context, output_bias_grad, gain_one_grad, shift_one_grad = first_back(
        place, tied, wi, grad_second, unit, inverse, gain_1, wo
    )
    outer_sums.send((), (grad_context,))
    inner_sums.send((), (grad_context,))
    inner_sums.fold()
    outer_sums.fold()
    tied = hold(grad_context, *outer_sums.sends, *inner_sums.sends)
    grad_query, grad_key, grad_value, query_bias_grad, value_bias_grad = attention_backward(
        place, query, key, value, tied, lse
    )
    inner_sums.send((), (grad_query,))
    outer_sums.send((), (grad_query,))
    inner_sums.fold()
    outer_sums.fold()
    lefts = [start, start, start, context]
    rights = [hold(grad_query, *outer_sums.sends, *inner_sums.sends), grad_key, grad_value, grad_attended]
    if staged:
        first_sums = Scatter(place, *weight_terms(place, lefts, rights, own_rows))
    else:
        first_sums = PlainScatter(
            jnp.concatenate([outer_sum(l, r) for l, r in zip(lefts, rights)], axis=1)
        )
    inner_sums.send((), first_sums.sends)
    outer_sums.send((), first_sums.sends)
    inner_sums.fold()
    grad_query = hold(grad_query, *first_sums.sends, *inner_sums.sends)
    input_grad, mask_grad = start_back(
        place, grad_first, (grad_query, grad_key, grad_value), weights, masked
    )
    first_sums.send((), (mask_grad,))
    first_sums.fold()
    inner_sums.send((), (mask_grad, *first_sums.sends))
    smalls = (
        query_bias_grad,
        value_bias_grad,
        output_bias_grad,
        outer_bias_grad,
        gain_one_grad,
        shift_one_grad,
        gain_two_grad,
        shift_two_grad,
        mask_grad,
        inner_bias_grad,
    )
    spots = [(i, 0, width, i, 0) for i in range(9)]
    spots += [(9, i * width, width, 9 + i, 0) for i in range(inner // width)]
    high = -(-(9 + inner // width) // 8) * 8
    packed = pack(place, smalls, spots, (high, width))
    total = Total(place, packed) if staged else PlainTotal(packed)
    got = total.step(first_sums.sends)
    first_sums.send((), (got,))
    got = total.step((), first_sums.sends)
    if staged:
        inner_sums.fold()
    first_sums.fold()
    inner_sums.send(first_sums.sends)
    first_sums.send((), (got,))
    got = total.step(first_sums.sends)
    first_sums.fold()
    first_sums.send((), (got,))
    got = total.step(first_sums.sends)
    first_sums.fold()
    total.step(first_sums.sends)
    first_sums.send((), (got,))
    packed = total.value
    order = (0, 1, 2, 9, 3, 4, 5, 6, 7, 8)
    firsts = first_sums.result
    return (
        layer_output,
        input_grad,
        *(firsts[:, i * width : (i + 1) * width] for i in range(4)),
        inner_sums.result,
        outer_sums.result,
        *(packed[9:9 + inner // width].reshape(-1) if i == 9 else packed[i] for i in order),
    )


def solution(mesh):
    placed = (
        P(("dp", "pair"), None),
        P(("dp", "pair"), None),
        P(("dp", "pair"), None),
        P(),
        P(("dp", "pair"), None),
        P(("dp", "pair"), None),
        P(("dp", "pair"), None),
        P(("dp", "pair"), None),
        P(("dp", "pair"), None),
        P(("dp", "pair"), None),
        P(),
        P(),
        P(),
        P(),
        P(),
        P(),
        P(),
        P(),
        P(),
        P(("dp", "pair"), None),
    )
    return jax.shard_map(
        on_device,
        mesh=mesh,
        in_specs=placed,
        out_specs=(
            P(("dp", "pair"), None),
            P(("dp", "pair"), None),
            P(("dp", "pair"), None),
            P(("dp", "pair"), None),
            P(("dp", "pair"), None),
            P(("dp", "pair"), None),
            P(("dp", "pair"), None),
            P(("dp", "pair"), None),
            P(),
            P(),
            P(),
            P(),
            P(),
            P(),
            P(),
            P(),
            P(),
            P(),
        ),
        check_vma=False,
    )
```

```python
import jax
import jax.numpy as jnp
from jax import lax
from jax.experimental import pallas as pl
from jax.experimental.pallas import tpu as pltpu
from jax.sharding import PartitionSpec as P

HD = 64
BOTH = ("dp", "pair")
LOW = jnp.bfloat16
COVER = 30


def hold(value, *others):
    others = [o for o in others if o is not None]
    return lax.optimization_barrier((value, *others))[0] if others else value


class Place:
    def __init__(self):
        self.chips = lax.axis_size("dp")
        fast = 1
        while (2 * fast) ** 3 <= self.chips:
            fast *= 2
        strides = []
        while (1 << len(strides)) < self.chips:
            strides.insert(0, self.chips >> (len(strides) + 1))
        strides = sorted(strides, reverse=True)
        self.fast = [b for b in strides if b < fast]
        self.mid = [b for b in strides if fast <= b < fast * fast]
        self.slow = [b for b in strides if b >= fast * fast]
        self.chip = lax.axis_index("dp")
        self.core = lax.axis_index("pair")
        self.where = jnp.stack([self.chip, self.core]).astype(jnp.int32)

    def swap(self, value, stride):
        return lax.ppermute(value, "dp", [(i, i ^ stride) for i in range(self.chips)])

    def swap_core(self, value):
        return lax.ppermute(value, "pair", [(0, 1), (1, 0)])


def kernel_call(body, grid, in_specs, out_specs, out_shape, cost, scratch=(), limit=None, cover=COVER):
    flops, moved, special = cost
    return pl.pallas_call(
        body,
        grid_spec=pltpu.PrefetchScalarGridSpec(
            num_scalar_prefetch=1,
            grid=grid,
            in_specs=in_specs,
            out_specs=out_specs,
            scratch_shapes=scratch,
        ),
        out_shape=out_shape,
        cost_estimate=pl.CostEstimate(
            flops=cover * flops, bytes_accessed=moved if flops == 0 else cover * moved, transcendentals=special
        ),
        compiler_params=pltpu.CompilerParams(vmem_limit_bytes=limit or 16 * 2**20),
    )


def pack(place, arrays, spots, shape):
    def body(at, *refs):
        out = refs[-1]
        for i, begin, width, row, column in spots:
            value = refs[i][:, begin : begin + width]
            out[row : row + value.shape[0], column : column + width] = value

    moved = 2 * sum(a.size * a.dtype.itemsize for a in arrays)
    return kernel_call(
        body,
        (1,),
        [pl.BlockSpec(a.shape, lambda i, at: (0, 0)) for a in arrays],
        pl.BlockSpec(shape, lambda i, at: (0, 0)),
        jax.ShapeDtypeStruct(shape, arrays[0].dtype),
        (0, moved, 0),
    )(place.where, *arrays)


class Gather:
    def __init__(self, place, rows):
        self.place = place
        self.slots = rows[None]
        self.left = place.slow + place.mid + place.fast
        self.right = place.slow + place.fast + place.mid
        self.stage = 0
        self.halves = None
        self.ready = ()

    def step(self, before=(), during=()):
        place, stage = self.place, self.stage
        self.stage += 1
        if stage < len(place.slow):
            value = hold(self.slots, *before)
            got = hold(place.swap(value, self.left[stage]), *during)
            self.slots = jnp.concatenate([value, got])
            self.ready = (self.slots,)
            if self.stage == len(place.slow):
                half = self.slots.shape[-1] // 2
                self.halves = self.ready = (self.slots[..., :half], self.slots[..., half:])
            return got
        if stage < len(self.left):
            l, r = (hold(v, *before) for v in self.halves)
            gl = hold(place.swap(l, self.left[stage]), *during)
            gr = hold(place.swap(r, self.right[stage]), *during)
            self.halves = self.ready = (jnp.concatenate([l, gl]), jnp.concatenate([r, gr]))
            if self.stage == len(self.left):
                self.stacked = jnp.stack(self.halves)
                self.ready = (self.stacked,)
            return gr
        self.own = hold(self.stacked, *before)
        self.other = hold(place.swap_core(self.own), *during)
        return self.other

    def done(self, parts):
        place = self.place
        _, chips, rows, half = self.own.shape
        orders = (self.left, self.right)

        def body(at, own, other, *outs):
            chip, core = at[0], at[1]
            for side in range(2):

                def put(j, carry):
                    to = chip
                    for i, stride in enumerate(orders[side]):
                        to = to ^ (((j >> i) & 1) * stride)
                    begin = 0
                    for out, width in zip(outs, parts):
                        cols = slice(side * width, (side + 1) * width)
                        out[2 * to + core, :, cols] = own[side, j, :, begin : begin + width]
                        out[2 * to + 1 - core, :, cols] = other[side, j, :, begin : begin + width]
                        begin += width
                    return carry

                lax.fori_loop(0, chips, put, 0)

        moved = 8 * chips * rows * half * 2
        whole = pl.BlockSpec((2, chips, rows, half), lambda i, at: (0, 0, 0, 0))
        outs = kernel_call(
            body,
            (1,),
            [whole, whole],
            [pl.BlockSpec((2 * chips, rows, 2 * w), lambda i, at: (0, 0, 0)) for w in parts],
            [jax.ShapeDtypeStruct((2 * chips, rows, 2 * w), LOW) for w in parts],
            (0, moved, 0),
        )(place.where, self.own, self.other)
        return [o.reshape(-1, o.shape[-1]) for o in outs]


def fold(place, keeps, gots, bits, join):
    sides = len(bits)
    deep = keeps[0].ndim == 4
    chips, rows, cols = keeps[0].shape[-3:]
    steps = next(s for s in (3, 2, 1) if rows % (8 * s) == 0)
    part = rows // steps

    def body(at, *refs):
        ins, outs = refs[: 2 * len(keeps)], refs[2 * len(keeps) :]
        for side in range(sides):
            for j in range(chips):
                if deep:
                    a, b = ins[0][side, j], ins[1][side, j]
                else:
                    a, b = ins[side][j], ins[len(keeps) + side][j]
                total = (a.astype(jnp.float32) + b.astype(jnp.float32)).astype(LOW)
                low = bits[side]
                to = (j // (2 * low)) * low + j % low
                goes = (j // low) % 2
                if join:
                    outs[goes][to, :, side * cols : (side + 1) * cols] = total
                else:
                    outs[goes * sides + side][to] = total

    if deep:
        ins = pl.BlockSpec((2, chips, part, cols), lambda i, at: (0, 0, i, 0))
    else:
        ins = pl.BlockSpec((chips, part, cols), lambda i, at: (0, i, 0))
    wide = cols * sides if join else cols
    count = 2 if join else 2 * sides
    outs = kernel_call(
        body,
        (steps,),
        [ins] * (2 * len(keeps)),
        [pl.BlockSpec((chips // 2, part, wide), lambda i, at: (0, i, 0))] * count,
        [jax.ShapeDtypeStruct((chips // 2, rows, wide), LOW)] * count,
        (0, 6 * sides * chips * rows * cols, 0),
    )(place.where, *keeps, *gots)
    return list(outs[: count // 2]), list(outs[count // 2 :])


class Scatter:
    def __init__(self, place, keep, send):
        self.place = place
        self.keeps, self.sends = [keep], [send]
        self.left = (place.slow + place.mid + place.fast)[::-1]
        self.right = (place.slow + place.fast + place.mid)[::-1]
        self.held = [sorted(self.left), sorted(self.right)]
        self.stage = -1
        self.result = None
        self.gots = None

    def fold(self):
        place = self.place
        if self.gots is not None:
            orders = (self.left, self.right)
            crossing = len(self.left) - len(place.slow)
            sides = 2 if self.stage <= crossing else 1
            bits = []
            for side in range(sides):
                stride = orders[side][self.stage]
                bits.append(1 << self.held[side].index(stride))
                self.held[side].remove(stride)
            join = self.stage == crossing
            self.keeps, self.sends = fold(place, self.keeps, self.gots, bits, join)
        return self.sends

    def send(self, before=(), during=()):
        place = self.place
        swaps = (
            [place.swap_core]
            if self.stage < 0
            else [lambda v, b=o[self.stage]: place.swap(v, b) for o in (self.left, self.right)]
        )
        self.gots = [
            hold(swap(hold(v, *before)), *during) for v, swap in zip(self.sends, swaps)
        ]
        self.stage += 1
        if self.stage == len(self.left):
            self.result = self.keeps[0][0].astype(jnp.float32) + self.gots[0][0].astype(jnp.float32)
        return self.gots


def weight_terms(place, lefts, rights, rows):
    chips = place.chips
    count = len(lefts)
    length, features = lefts[0].shape
    joined = not isinstance(rights, list)
    width = rights.shape[1] // count if joined else rights[0].shape[1]
    per = count // 2
    unique = []
    for l in lefts:
        if not any(l is u for u in unique):
            unique.append(l)
    which = [next(i for i, u in enumerate(unique) if u is l) for l in lefts]
    rights = [rights] if joined else rights

    def body(at, *refs):
        ins, (keep, send) = refs[:-2], refs[-2:]
        t = pl.program_id(0)
        chip, core = at[0], at[1]

        def one(left, right):
            total = lax.dot_general(
                left[...], right[...], (((0,), (0,)), ((), ())), preferred_element_type=jnp.float32
            )
            for c in range(chips):
                to = c ^ chip
                a = total[2 * c * rows : (2 * c + 1) * rows].astype(LOW)
                b = total[(2 * c + 1) * rows : (2 * c + 2) * rows].astype(LOW)
                keep[0, to] = jnp.where(core == 0, a, b)
                send[0, to] = jnp.where(core == 0, b, a)

        if joined:
            one(ins[0], ins[1])
        else:
            for k in range(count):
                pl.when(t == k)(lambda k=k: one(ins[which[k]], ins[len(unique) + k]))

    block = pl.BlockSpec((1, chips, rows, width), lambda t, at: (t // per, 0, 0, t % per))
    shape = jax.ShapeDtypeStruct((2, chips, rows, width * per), LOW)
    fixed = pl.BlockSpec((length, width), lambda t, at: (0, 0))
    return kernel_call(
        body,
        (count,),
        [pl.BlockSpec((length, features), lambda t, at: (0, 0)) for _ in unique]
        + ([pl.BlockSpec((length, width), lambda t, at: (0, t))] if joined else [fixed] * count),
        [block, block],
        [shape, shape],
        (2 * count * length * features * width, 4 * count * features * width, 0),
    )(place.where, *unique, *rights)


def weight_terms_tall(place, left, right, rows):
    chips = place.chips
    length, features = left.shape
    width = right.shape[1]
    tiles = 4
    group = chips // tiles

    def body(at, left_ref, right_ref, keep, send):
        chip, core = at[0], at[1]
        total = lax.dot_general(
            left_ref[...], right_ref[...], (((0,), (0,)), ((), ())), preferred_element_type=jnp.float32
        )
        for c in range(group):
            to = c ^ (chip % group)
            a = total[2 * c * rows : (2 * c + 1) * rows].astype(LOW)
            b = total[(2 * c + 1) * rows : (2 * c + 2) * rows].astype(LOW)
            own, other = jnp.where(core == 0, a, b), jnp.where(core == 0, b, a)
            for side in range(2):
                cols = slice(side * (width // 2), (side + 1) * (width // 2))
                keep[side, to] = own[:, cols]
                send[side, to] = other[:, cols]

    block = pl.BlockSpec((2, group, rows, width // 2), lambda t, at: (0, t, 0, 0))
    shape = jax.ShapeDtypeStruct((2, chips, rows, width // 2), LOW)
    return kernel_call(
        body,
        (tiles,),
        [
            pl.BlockSpec((length, features // tiles), lambda t, at: (0, t ^ (at[0] // group))),
            pl.BlockSpec((length, width), lambda t, at: (0, 0)),
        ],
        [block, block],
        [shape, shape],
        (2 * length * features * width, 4 * features * width, 0),
    )(place.where, left, right)


class Total:
    def __init__(self, place, value):
        self.place, self.value = place, value
        self.strides = [0] + place.fast + place.mid + place.slow

    def step(self, before=(), during=()):
        if not self.strides:
            return None
        value = hold(self.value, *before)
        stride = self.strides.pop(0)
        got = hold(self.place.swap(value, stride) if stride else self.place.swap_core(value), *during)
        self.value = value + got
        return got


def attention_forward(place, start, weights, query_bias, value_bias, seqs):
    rows, width = start.shape
    length = rows // seqs
    cols = 4 * HD
    groups = width // cols

    def body(at, start, wq, wk, wv, qb, vb, query, key, value, context, lse):
        x = start[...]
        dot = lambda l, r: jnp.dot(l, r, preferred_element_type=jnp.float32)
        query[...] = (dot(x, wq[...]) + qb[...]).astype(LOW)
        key[...] = dot(x, wk[...]).astype(LOW)
        value[...] = (dot(x, wv[...]) + vb[...]).astype(LOW)
        lane = lax.broadcasted_iota(jnp.int32, (length, 2 * HD), 1)
        for pair in range(2):
            at_cols = slice(pair * 2 * HD, (pair + 1) * 2 * HD)
            q, k = query[:, at_cols], key[:, at_cols]
            v_across = value[:, at_cols].T
            mixed = []
            for h in range(2):
                mine = (lane < HD) if h == 0 else (lane >= HD)
                q_mine = jnp.where(mine, q * jnp.asarray(HD**-0.5, LOW), jnp.zeros_like(q))
                scores = lax.dot_general(
                    k, q_mine, (((1,), (1,)), ((), ())), preferred_element_type=jnp.float32
                )
                most = jnp.max(scores, axis=0, keepdims=True)
                raised = jnp.exp(scores - most)
                total = jnp.sum(raised, axis=0, keepdims=True)
                probs = (raised * (1.0 / total)).astype(LOW)
                mixed.append(dot(v_across[h * HD : (h + 1) * HD], probs))
                lse[0, 0, 2 * pair + h : 2 * pair + h + 1, :] = most + jnp.log(total)
            context[:, at_cols] = jnp.concatenate(mixed, axis=0).T.astype(LOW)

    block = pl.BlockSpec((length, cols), lambda s, g, at: (s, g))
    weight = pl.BlockSpec((width, cols), lambda s, g, at: (0, g))
    bias = pl.BlockSpec((1, cols), lambda s, g, at: (0, g))
    table = jax.ShapeDtypeStruct((rows, width), LOW)
    return kernel_call(
        body,
        (seqs, groups),
        [pl.BlockSpec((length, width), lambda s, g, at: (s, 0)), weight, weight, weight, bias, bias],
        [block] * 4 + [pl.BlockSpec((1, 1, 4, length), lambda s, g, at: (s, g, 0, 0))],
        [table] * 4 + [jax.ShapeDtypeStruct((seqs, groups, 4, length), jnp.float32)],
        (6 * rows * width * width, 6 * width * width, seqs * groups * 4 * length * length),
    )(place.where, start, *weights, query_bias, value_bias)


def attention_backward(place, query, key, value, grad_context, lse):
    rows, width = query.shape
    seqs, groups, _, length = lse.shape
    cols = 4 * HD

    def body(at, query, key, value, grad, lse, dq, dk, dv, dq_sum, dv_sum):
        dot = lambda l, r: jnp.dot(l, r, preferred_element_type=jnp.float32)
        dot_t = lambda l, r: lax.dot_general(
            l, r, (((1,), (1,)), ((), ())), preferred_element_type=jnp.float32
        )
        lane = lax.broadcasted_iota(jnp.int32, (length, 2 * HD), 1)
        for pair in range(2):
            at_cols = slice(pair * 2 * HD, (pair + 1) * 2 * HD)
            q, k, v, g = query[:, at_cols], key[:, at_cols], value[:, at_cols], grad[:, at_cols]
            k_across = k.T
            dqs, dks, dvs = [], [], []
            for h in range(2):
                mine = (lane < HD) if h == 0 else (lane >= HD)
                none = jnp.zeros_like(q)
                scaled = jnp.where(mine, q * jnp.asarray(HD**-0.5, LOW), none)
                scores = dot_t(k, scaled)
                probs = jnp.exp(scores - lse[0, 0, 2 * pair + h : 2 * pair + h + 1, :])
                grad_probs = dot_t(v, jnp.where(mine, g, none))
                dvs.append(dot(probs.astype(LOW), g))
                inner = jnp.sum(probs * grad_probs, axis=0, keepdims=True)
                grad_scores = (probs * (grad_probs - inner)).astype(LOW)
                dks.append(dot(grad_scores, q))
                dqs.append(dot(k_across[h * HD : (h + 1) * HD], grad_scores))
            scale = HD**-0.5
            dq_low = (jnp.concatenate(dqs, axis=0).T * scale).astype(LOW)
            dk_low = (jnp.where(lane < HD, dks[0], dks[1]) * scale).astype(LOW)
            dv_low = jnp.where(lane < HD, dvs[0], dvs[1]).astype(LOW)
            dq[:, at_cols], dk[:, at_cols], dv[:, at_cols] = dq_low, dk_low, dv_low
            for total, term in ((dq_sum, dq_low), (dv_sum, dv_low)):
                term = jnp.sum(term.astype(jnp.float32), axis=0, keepdims=True)

                @pl.when(pl.program_id(1) == 0)
                def _(total=total, term=term):
                    total[:, at_cols] = term

                @pl.when(pl.program_id(1) > 0)
                def _(total=total, term=term):
                    total[:, at_cols] += term

    block = pl.BlockSpec((length, cols), lambda g, s, at: (s, g))
    total = pl.BlockSpec((1, cols), lambda g, s, at: (0, g))
    table = jax.ShapeDtypeStruct((rows, width), LOW)
    sums = jax.ShapeDtypeStruct((1, width), jnp.float32)
    return kernel_call(
        body,
        (groups, seqs),
        [block] * 4 + [pl.BlockSpec((1, 1, 4, length), lambda g, s, at: (s, g, 0, 0))],
        [block] * 3 + [total] * 2,
        [table] * 3 + [sums] * 2,
        (10 * rows * length * width, 14 * rows * width, rows * length * width // HD),
    )(place.where, query, key, value, grad_context, lse)


def normalised(value):
    centered = value - jnp.mean(value, axis=-1, keepdims=True)
    inverse = lax.rsqrt(jnp.mean(centered * centered, axis=-1, keepdims=True) + 1e-12)
    return centered * inverse, inverse


def normalised_back(grad, unit, inverse, gain):
    inner = grad * gain
    mean = jnp.mean(inner, axis=-1, keepdims=True)
    along = jnp.mean(inner * unit, axis=-1, keepdims=True)
    return (
        inverse * (inner - mean - unit * along),
        jnp.sum(grad * unit, axis=0, keepdims=True),
        jnp.sum(grad, axis=0, keepdims=True),
    )


def feed_in(place, start, context, wo, output_bias, gain, shift, wi, inner_bias):
    rows, width = start.shape
    inner = wi.shape[1]
    tile = width

    def body(at, start, context, wo, ob, gain, shift, wi, ib, unit, inverse, normed_low, active, slope):
        @pl.when(pl.program_id(0) == 0)
        def _():
            first = (
                start[...].astype(jnp.float32)
                + jnp.dot(context[...], wo[...], preferred_element_type=jnp.float32)
                + ob[...]
            )
            u, i = normalised(first)
            unit[...] = u
            inverse[...] = i
            normed_low[...] = (u * gain[...] + shift[...]).astype(LOW)

        for part in range(4):
            cut = slice(part * tile // 4, (part + 1) * tile // 4)
            hidden = (
                jnp.dot(normed_low[...], wi[:, cut], preferred_element_type=jnp.float32) + ib[:, cut]
            )
            below = 0.5 + 0.5 * lax.erf(hidden * 0.7071067811865476)
            active[:, cut] = (hidden * below).astype(LOW)
            bell = jnp.exp(hidden * hidden * -0.5) * 0.3989422804014327
            slope[:, cut] = (below + hidden * bell).astype(LOW)

    keep = lambda a: pl.BlockSpec(a.shape, lambda t, at: (0, 0))
    column = pl.BlockSpec((rows, tile), lambda t, at: (0, t))
    shapes = [
        jax.ShapeDtypeStruct((rows, width), jnp.float32),
        jax.ShapeDtypeStruct((rows, 1), jnp.float32),
        jax.ShapeDtypeStruct((rows, width), LOW),
        jax.ShapeDtypeStruct((rows, inner), LOW),
        jax.ShapeDtypeStruct((rows, inner), LOW),
    ]
    ins = (start, context, wo, output_bias, gain, shift)
    return kernel_call(
        body,
        (inner // tile,),
        [keep(a) for a in ins]
        + [
            pl.BlockSpec((width, tile), lambda t, at: (0, t)),
            pl.BlockSpec((1, tile), lambda t, at: (0, t)),
        ],
        [keep(s) for s in shapes[:3]] + [column, column],
        shapes,
        (2 * rows * width * (width + inner), 2 * width * inner, 2 * rows * inner),
    )(place.where, *ins, wi, inner_bias)


def feed_out(place, active, wu, outer_bias, unit, gain_one, shift_one, gain, shift, cotangent, wanted):
    rows, width = unit.shape
    inner = active.shape[1]
    tile = width
    steps = inner // tile

    def body(at, active, wu, ob, unit, g1, s1, g2, s2, cot, wanted, out, grad, branch, ob_g, g2_g, s2_g, total):
        t = pl.program_id(0)
        term = jnp.dot(active[...], wu[...], preferred_element_type=jnp.float32)

        @pl.when(t == 0)
        def _():
            total[...] = unit[...] * g1[...] + s1[...] + ob[...] + term

        @pl.when(t > 0)
        def _():
            total[...] += term

        @pl.when(t == steps - 1)
        def _():
            u, i = normalised(total[...])
            out[...] = (u * g2[...] + s2[...]).astype(LOW)
            grad_out = cot[...].astype(jnp.float32) * wanted[...]
            back, gain_grad, shift_grad = normalised_back(grad_out, u, i, g2[...])
            grad[...] = back
            low = back.astype(LOW)
            branch[...] = low
            ob_g[...] = jnp.sum(low.astype(jnp.float32), axis=0, keepdims=True)
            g2_g[...] = gain_grad
            s2_g[...] = shift_grad

    keep = lambda a: pl.BlockSpec(a.shape, lambda t, at: (0, 0))
    row = jax.ShapeDtypeStruct((1, width), jnp.float32)
    shapes = [
        jax.ShapeDtypeStruct((rows, width), LOW),
        jax.ShapeDtypeStruct((rows, width), jnp.float32),
        jax.ShapeDtypeStruct((rows, width), LOW),
        row,
        row,
        row,
    ]
    ins = (outer_bias, unit, gain_one, shift_one, gain, shift, cotangent, wanted)
    return kernel_call(
        body,
        (steps,),
        [
            pl.BlockSpec((rows, tile), lambda t, at: (0, t)),
            pl.BlockSpec((tile, width), lambda t, at: (t, 0)),
        ]
        + [keep(a) for a in ins],
        [keep(s) for s in shapes],
        shapes,
        (2 * rows * width * inner, 2 * width * inner, 0),
        [pltpu.VMEM((rows, width), jnp.float32)],
    )(place.where, active, wu, *ins)


def hidden_back(place, grad_branch, wu, slope):
    rows, width = grad_branch.shape
    inner = wu.shape[0]
    tile = width

    def body(at, grad, wu, slope, out, sums):
        back = lax.dot_general(
            grad[...], wu[...], (((1,), (1,)), ((), ())), preferred_element_type=jnp.float32
        )
        low = (back * slope[...].astype(jnp.float32)).astype(LOW)
        out[...] = low
        sums[...] = jnp.sum(low.astype(jnp.float32), axis=0, keepdims=True)

    column = pl.BlockSpec((rows, tile), lambda t, at: (0, t))
    return kernel_call(
        body,
        (inner // tile,),
        [
            pl.BlockSpec((rows, width), lambda t, at: (0, 0)),
            pl.BlockSpec((tile, width), lambda t, at: (t, 0)),
            column,
        ],
        [column, pl.BlockSpec((1, tile), lambda t, at: (0, t))],
        [jax.ShapeDtypeStruct((rows, inner), LOW), jax.ShapeDtypeStruct((1, inner), jnp.float32)],
        (2 * rows * width * inner, 2 * width * inner, 0),
    )(place.where, grad_branch, wu, slope)


def first_back(place, grad_hidden, wi, grad_second, unit, inverse, gain, wo):
    rows, width = grad_second.shape
    inner = wi.shape[1]
    tile = width
    steps = inner // tile

    def body(at, gh, wi, second, unit, inverse, gain, wo, first, low_out, context, ob_g, g_g, s_g, total):
        t = pl.program_id(0)
        term = lax.dot_general(
            gh[...], wi[...], (((1,), (1,)), ((), ())), preferred_element_type=jnp.float32
        )

        @pl.when(t == 0)
        def _():
            total[...] = second[...] + term

        @pl.when(t > 0)
        def _():
            total[...] += term

        @pl.when(t == steps - 1)
        def _():
            back, gain_grad, shift_grad = normalised_back(
                total[...], unit[...], inverse[...], gain[...]
            )
            first[...] = back
            low = back.astype(LOW)
            low_out[...] = low
            ob_g[...] = jnp.sum(low.astype(jnp.float32), axis=0, keepdims=True)
            g_g[...] = gain_grad
            s_g[...] = shift_grad
            context[...] = lax.dot_general(
                low, wo[...], (((1,), (1,)), ((), ())), preferred_element_type=jnp.float32
            ).astype(LOW)

    keep = lambda a: pl.BlockSpec(a.shape, lambda t, at: (0, 0))
    row = jax.ShapeDtypeStruct((1, width), jnp.float32)
    shapes = [
        jax.ShapeDtypeStruct((rows, width), jnp.float32),
        jax.ShapeDtypeStruct((rows, width), LOW),
        jax.ShapeDtypeStruct((rows, width), LOW),
        row,
        row,
        row,
    ]
    ins = (grad_second, unit, inverse, gain, wo)
    return kernel_call(
        body,
        (steps,),
        [
            pl.BlockSpec((rows, tile), lambda t, at: (0, t)),
            pl.BlockSpec((width, tile), lambda t, at: (0, t)),
        ]
        + [keep(a) for a in ins],
        [keep(s) for s in shapes],
        shapes,
        (2 * rows * width * (inner + width), 2 * width * inner, 0),
        [pltpu.VMEM((rows, width), jnp.float32)],
    )(place.where, grad_hidden, wi, *ins)


def start_back(place, grad_first, grads, weights, masked):
    rows, width = grad_first.shape

    def body(at, first, dq, dk, dv, wq, wk, wv, masked, out, sums):
        total = first[...]
        for grad, weight in ((dq, wq), (dk, wk), (dv, wv)):
            total += lax.dot_general(
                grad[...], weight[...], (((1,), (1,)), ((), ())), preferred_element_type=jnp.float32
            )
        hidden = masked[...] > 0.0
        out[...] = jnp.where(hidden, 0.0, total).astype(LOW)
        sums[...] = jnp.sum(jnp.where(hidden, total, 0.0), axis=0, keepdims=True)

    ins = (grad_first, *grads, *weights, masked)
    shapes = [jax.ShapeDtypeStruct((rows, width), LOW), jax.ShapeDtypeStruct((1, width), jnp.float32)]
    return kernel_call(
        body,
        (1,),
        [pl.BlockSpec(a.shape, lambda t, at: (0, 0)) for a in ins],
        [pl.BlockSpec(s.shape, lambda t, at: (0, 0)) for s in shapes],
        shapes,
        (6 * rows * width * width, 6 * width * width, 0),
    )(place.where, *ins)


class PlainGather:
    def __init__(self, rows):
        self.rows = rows
        self.ready = ()

    def step(self, before=(), during=()):
        return None

    def done(self, parts):
        whole = lax.all_gather(self.rows, BOTH, axis=0, tiled=True)
        half = whole.shape[1] // 2
        outs, begin = [], 0
        for width in parts:
            outs.append(
                jnp.concatenate(
                    [whole[:, s * half + begin : s * half + begin + width] for s in range(2)], axis=1
                )
            )
            begin += width
        return outs


class PlainScatter:
    def __init__(self, term):
        self.result = lax.psum_scatter(term, BOTH, scatter_dimension=0, tiled=True)
        self.sends = ()

    def fold(self):
        return ()

    def send(self, before=(), during=()):
        return ()


class PlainTotal:
    def __init__(self, value):
        self.value = lax.psum(value, BOTH)

    def step(self, before=(), during=()):
        return None


def outer_sum(left, right):
    return jnp.einsum("rd,re->de", left, right, preferred_element_type=jnp.float32)


def halves(place, arrays):
    spots, column = [], 0
    for side in range(2):
        for i, a in enumerate(arrays):
            half = a.shape[1] // 2
            spots.append((i, side * half, half, 0, column))
            column += half
    return pack(place, arrays, spots, (arrays[0].shape[0], column))


def on_device(
    tokens,
    span_starts,
    span_lengths,
    mask_embed,
    query_weight,
    key_weight,
    value_weight,
    output_weight,
    inner_weight,
    outer_weight,
    query_bias,
    value_bias,
    output_bias,
    inner_bias,
    outer_bias,
    gain_one,
    shift_one,
    gain_two,
    shift_two,
    cotangent,
):
    rows, width = tokens.shape
    seqs = span_starts.shape[0]
    length = rows // seqs
    inner = inner_weight.shape[1]
    own_rows, own_tall = query_weight.shape[0], outer_weight.shape[0]
    place = Place()
    staged = own_rows % 8 == 0 and place.chips & (place.chips - 1) == 0
    gather = (lambda piece: Gather(place, piece)) if staged else PlainGather

    first_gather = gather(halves(place, (query_weight, key_weight, value_weight)))
    inner_gather = gather(halves(place, (output_weight, inner_weight)))
    outer_gather = gather(outer_weight)
    first_gather.step()
    places = jnp.arange(length, dtype=jnp.int32)[None, :, None]
    begins = span_starts[:, None, :]
    finish = begins + span_lengths[:, None, :]
    masked = jnp.any((places >= begins) & (places < finish), axis=2)
    edges = jnp.any((places == begins - 1) | (places == finish), axis=2)
    masked = masked.reshape(rows)
    wanted = (masked | edges.reshape(rows)).astype(jnp.float32)[:, None]
    start = jnp.where(masked[:, None], mask_embed[None, :], tokens)
    masked = masked.astype(jnp.float32)[:, None]
    vectors = (
        query_bias,
        value_bias,
        output_bias,
        inner_bias,
        outer_bias,
        gain_one,
        shift_one,
        gain_two,
        shift_two,
    )
    vectors = tuple(v[None] for v in vectors)
    query_row, value_row, output_row, inner_row, outer_row, gain_1, shift_1, gain_2, shift_2 = vectors
    before = first_gather.ready
    first_gather.step(during=(*vectors, start, masked, wanted))
    inner_gather.step(before, first_gather.ready)
    before = first_gather.ready
    first_gather.step()
    inner_gather.step(before, first_gather.ready)
    first_gather.step()
    before = inner_gather.ready
    inner_gather.step(first_gather.ready)
    outer_gather.step(before, inner_gather.ready)
    got = first_gather.step()
    weights = first_gather.done((width // 2,) * 3)
    query, key, value, context, lse = attention_forward(
        place, hold(start, *inner_gather.ready, *outer_gather.ready), weights, query_row, value_row, seqs
    )
    outer_gather.step(inner_gather.ready, (context,))
    inner_gather.step((got,), (context, *outer_gather.ready))
    got = inner_gather.step((context,))
    outer_gather.step(inner_gather.ready, (got,))
    wo, wi = inner_gather.done((width // 2, inner // 2))
    unit, inverse, normed_low, active, slope = feed_in(
        place, start, hold(context, *outer_gather.ready), wo, output_row, gain_1, shift_1, wi, inner_row
    )
    outer_gather.step((), (active,))
    outer_gather.step()
    (wu,) = outer_gather.done((width // 2,))
    layer_output, grad_second, grad_branch, outer_bias_grad, gain_two_grad, shift_two_grad = feed_out(
        place, active, wu, outer_row, unit, gain_1, shift_1, gain_2, shift_2, cotangent, wanted
    )
    if staged:
        outer_sums = Scatter(place, *weight_terms_tall(place, active, grad_branch, own_tall))
    else:
        outer_sums = PlainScatter(outer_sum(active, grad_branch))
    grad_hidden, inner_bias_grad = hidden_back(place, hold(grad_branch, *outer_sums.sends), wu, slope)
    outer_sums.send((), (grad_hidden,))
    outer_sums.fold()
    if staged:
        tiles = inner // width
        grad_tied = hold(grad_hidden, *outer_sums.sends)
        inner_sums = Scatter(place, *weight_terms(place, [normed_low] * tiles, grad_tied, own_rows))
    else:
        inner_sums = PlainScatter(outer_sum(normed_low, grad_hidden))
    outer_sums.send((), inner_sums.sends)
    outer_sums.fold()
    tied = hold(grad_hidden, *inner_sums.sends, *outer_sums.sends)
    grad_first, grad_attended, grad_context, output_bias_grad, gain_one_grad, shift_one_grad = first_back(
        place, tied, wi, grad_second, unit, inverse, gain_1, wo
    )
    outer_sums.send((), (grad_context,))
    inner_sums.send((), (grad_context,))
    inner_sums.fold()
    outer_sums.fold()
    tied = hold(grad_context, *outer_sums.sends, *inner_sums.sends)
    grad_query, grad_key, grad_value, query_bias_grad, value_bias_grad = attention_backward(
        place, query, key, value, tied, lse
    )
    inner_sums.send((), (grad_query,))
    outer_sums.send((), (grad_query,))
    inner_sums.fold()
    outer_sums.fold()
    lefts = [start, start, start, context]
    rights = [hold(grad_query, *outer_sums.sends, *inner_sums.sends), grad_key, grad_value, grad_attended]
    if staged:
        first_sums = Scatter(place, *weight_terms(place, lefts, rights, own_rows))
    else:
        first_sums = PlainScatter(
            jnp.concatenate([outer_sum(l, r) for l, r in zip(lefts, rights)], axis=1)
        )
    inner_sums.send((), first_sums.sends)
    outer_sums.send((), first_sums.sends)
    inner_sums.fold()
    grad_query = hold(grad_query, *first_sums.sends, *inner_sums.sends)
    input_grad, mask_grad = start_back(
        place, grad_first, (grad_query, grad_key, grad_value), weights, masked
    )
    first_sums.send((), (mask_grad,))
    first_sums.fold()
    tied = (mask_grad, *first_sums.sends)
    late = inner_sums.send((), tied)
    inner_sums.fold()
    smalls = (
        query_bias_grad,
        value_bias_grad,
        output_bias_grad,
        outer_bias_grad,
        gain_one_grad,
        shift_one_grad,
        gain_two_grad,
        shift_two_grad,
        mask_grad,
        inner_bias_grad,
    )
    spots = [(i, 0, width, i, 0) for i in range(9)]
    spots += [(9, i * width, width, 9 + i, 0) for i in range(inner // width)]
    high = -(-(9 + inner // width) // 8) * 8
    smalls = (hold(query_bias_grad, *inner_sums.sends), *smalls[1:])
    packed = pack(place, smalls, spots, (high, width))
    total = Total(place, packed) if staged else PlainTotal(packed)
    got = total.step(first_sums.sends)
    got = total.step(first_sums.sends)
    late = inner_sums.send(first_sums.sends)
    first_sums.send((), (got, *late))
    first_sums.fold()
    got = total.step(first_sums.sends)
    first_sums.send((), (got,))
    first_sums.fold()
    got = total.step(first_sums.sends)
    first_sums.send((), (got,))
    first_sums.fold()
    total.step(first_sums.sends)
    first_sums.send()
    packed = total.value
    order = (0, 1, 2, 9, 3, 4, 5, 6, 7, 8)
    firsts = first_sums.result
    return (
        layer_output,
        input_grad,
        *(firsts[:, i * width : (i + 1) * width] for i in range(4)),
        inner_sums.result,
        outer_sums.result,
        *(packed[9:9 + inner // width].reshape(-1) if i == 9 else packed[i] for i in order),
    )


def solution(mesh):
    placed = (
        P(("dp", "pair"), None),
        P(("dp", "pair"), None),
        P(("dp", "pair"), None),
        P(),
        P(("dp", "pair"), None),
        P(("dp", "pair"), None),
        P(("dp", "pair"), None),
        P(("dp", "pair"), None),
        P(("dp", "pair"), None),
        P(("dp", "pair"), None),
        P(),
        P(),
        P(),
        P(),
        P(),
        P(),
        P(),
        P(),
        P(),
        P(("dp", "pair"), None),
    )
    return jax.shard_map(
        on_device,
        mesh=mesh,
        in_specs=placed,
        out_specs=(
            P(("dp", "pair"), None),
            P(("dp", "pair"), None),
            P(("dp", "pair"), None),
            P(("dp", "pair"), None),
            P(("dp", "pair"), None),
            P(("dp", "pair"), None),
            P(("dp", "pair"), None),
            P(("dp", "pair"), None),
            P(),
            P(),
            P(),
            P(),
            P(),
            P(),
            P(),
            P(),
            P(),
            P(),
        ),
        check_vma=False,
    )
```

```python
import jax
import jax.numpy as jnp
from jax import lax
from jax.experimental import pallas as pl
from jax.experimental.pallas import tpu as pltpu
from jax.sharding import PartitionSpec as P

HD = 64
BOTH = ("dp", "pair")
LOW = jnp.bfloat16
COVER = 30


def hold(value, *others):
    others = [o for o in others if o is not None]
    return lax.optimization_barrier((value, *others))[0] if others else value


class Place:
    def __init__(self):
        self.chips = lax.axis_size("dp")
        fast = 1
        while (2 * fast) ** 3 <= self.chips:
            fast *= 2
        strides = []
        while (1 << len(strides)) < self.chips:
            strides.insert(0, self.chips >> (len(strides) + 1))
        strides = sorted(strides, reverse=True)
        self.fast = [b for b in strides if b < fast]
        self.mid = [b for b in strides if fast <= b < fast * fast]
        self.slow = [b for b in strides if b >= fast * fast]
        self.chip = lax.axis_index("dp")
        self.core = lax.axis_index("pair")
        self.where = jnp.stack([self.chip, self.core]).astype(jnp.int32)

    def swap(self, value, stride):
        return lax.ppermute(value, "dp", [(i, i ^ stride) for i in range(self.chips)])

    def swap_core(self, value):
        return lax.ppermute(value, "pair", [(0, 1), (1, 0)])


def kernel_call(body, grid, in_specs, out_specs, out_shape, cost, scratch=(), limit=None, cover=COVER):
    flops, moved, special = cost
    return pl.pallas_call(
        body,
        grid_spec=pltpu.PrefetchScalarGridSpec(
            num_scalar_prefetch=1,
            grid=grid,
            in_specs=in_specs,
            out_specs=out_specs,
            scratch_shapes=scratch,
        ),
        out_shape=out_shape,
        cost_estimate=pl.CostEstimate(
            flops=cover * flops, bytes_accessed=moved if flops == 0 else cover * moved, transcendentals=special
        ),
        compiler_params=pltpu.CompilerParams(vmem_limit_bytes=limit or 16 * 2**20),
    )


def pack(place, arrays, spots, shape):
    def body(at, *refs):
        out = refs[-1]
        for i, begin, width, row, column in spots:
            value = refs[i][:, begin : begin + width]
            out[row : row + value.shape[0], column : column + width] = value

    moved = 2 * sum(a.size * a.dtype.itemsize for a in arrays)
    return kernel_call(
        body,
        (1,),
        [pl.BlockSpec(a.shape, lambda i, at: (0, 0)) for a in arrays],
        pl.BlockSpec(shape, lambda i, at: (0, 0)),
        jax.ShapeDtypeStruct(shape, arrays[0].dtype),
        (0, moved, 0),
    )(place.where, *arrays)


class Gather:
    def __init__(self, place, rows):
        self.place = place
        self.slots = rows[None]
        self.left = place.slow + place.mid + place.fast
        self.right = place.slow + place.fast + place.mid
        self.stage = 0
        self.halves = None
        self.ready = ()

    def step(self, before=(), during=()):
        place, stage = self.place, self.stage
        self.stage += 1
        if stage < len(place.slow):
            value = hold(self.slots, *before)
            got = hold(place.swap(value, self.left[stage]), *during)
            self.slots = jnp.concatenate([value, got])
            self.ready = (self.slots,)
            if self.stage == len(place.slow):
                half = self.slots.shape[-1] // 2
                self.halves = self.ready = (self.slots[..., :half], self.slots[..., half:])
            return got
        if stage < len(self.left):
            l, r = (hold(v, *before) for v in self.halves)
            gl = hold(place.swap(l, self.left[stage]), *during)
            gr = hold(place.swap(r, self.right[stage]), *during)
            self.halves = self.ready = (jnp.concatenate([l, gl]), jnp.concatenate([r, gr]))
            if self.stage == len(self.left):
                self.stacked = jnp.stack(self.halves)
                self.ready = (self.stacked,)
            return gr
        self.own = hold(self.stacked, *before)
        self.other = hold(place.swap_core(self.own), *during)
        return self.other

    def done(self, parts):
        place = self.place
        _, chips, rows, half = self.own.shape
        orders = (self.left, self.right)

        def body(at, own, other, *outs):
            chip, core = at[0], at[1]
            for side in range(2):

                def put(j, carry):
                    to = chip
                    for i, stride in enumerate(orders[side]):
                        to = to ^ (((j >> i) & 1) * stride)
                    begin = 0
                    for out, width in zip(outs, parts):
                        cols = slice(side * width, (side + 1) * width)
                        out[2 * to + core, :, cols] = own[side, j, :, begin : begin + width]
                        out[2 * to + 1 - core, :, cols] = other[side, j, :, begin : begin + width]
                        begin += width
                    return carry

                lax.fori_loop(0, chips, put, 0)

        moved = 8 * chips * rows * half * 2
        whole = pl.BlockSpec((2, chips, rows, half), lambda i, at: (0, 0, 0, 0))
        outs = kernel_call(
            body,
            (1,),
            [whole, whole],
            [pl.BlockSpec((2 * chips, rows, 2 * w), lambda i, at: (0, 0, 0)) for w in parts],
            [jax.ShapeDtypeStruct((2 * chips, rows, 2 * w), LOW) for w in parts],
            (0, moved, 0),
        )(place.where, self.own, self.other)
        return [o.reshape(-1, o.shape[-1]) for o in outs]


def fold(place, keeps, gots, bits, join):
    sides = len(bits)
    deep = keeps[0].ndim == 4
    chips, rows, cols = keeps[0].shape[-3:]
    steps = next(s for s in (3, 2, 1) if rows % (8 * s) == 0)
    part = rows // steps

    def body(at, *refs):
        ins, outs = refs[: 2 * len(keeps)], refs[2 * len(keeps) :]
        for side in range(sides):
            for j in range(chips):
                if deep:
                    a, b = ins[0][side, j], ins[1][side, j]
                else:
                    a, b = ins[side][j], ins[len(keeps) + side][j]
                total = (a.astype(jnp.float32) + b.astype(jnp.float32)).astype(LOW)
                low = bits[side]
                to = (j // (2 * low)) * low + j % low
                goes = (j // low) % 2
                if join:
                    outs[goes][to, :, side * cols : (side + 1) * cols] = total
                else:
                    outs[goes * sides + side][to] = total

    if deep:
        ins = pl.BlockSpec((2, chips, part, cols), lambda i, at: (0, 0, i, 0))
    else:
        ins = pl.BlockSpec((chips, part, cols), lambda i, at: (0, i, 0))
    wide = cols * sides if join else cols
    count = 2 if join else 2 * sides
    outs = kernel_call(
        body,
        (steps,),
        [ins] * (2 * len(keeps)),
        [pl.BlockSpec((chips // 2, part, wide), lambda i, at: (0, i, 0))] * count,
        [jax.ShapeDtypeStruct((chips // 2, rows, wide), LOW)] * count,
        (0, 6 * sides * chips * rows * cols, 0),
    )(place.where, *keeps, *gots)
    return list(outs[: count // 2]), list(outs[count // 2 :])


class Scatter:
    def __init__(self, place, keep, send):
        self.place = place
        self.keeps, self.sends = [keep], [send]
        self.left = (place.slow + place.mid + place.fast)[::-1]
        self.right = (place.slow + place.fast + place.mid)[::-1]
        self.held = [sorted(self.left), sorted(self.right)]
        self.stage = -1
        self.result = None
        self.gots = None

    def fold(self):
        place = self.place
        if self.gots is not None:
            orders = (self.left, self.right)
            crossing = len(self.left) - len(place.slow)
            sides = 2 if self.stage <= crossing else 1
            bits = []
            for side in range(sides):
                stride = orders[side][self.stage]
                bits.append(1 << self.held[side].index(stride))
                self.held[side].remove(stride)
            join = self.stage == crossing
            self.keeps, self.sends = fold(place, self.keeps, self.gots, bits, join)
        return self.sends

    def send(self, before=(), during=()):
        place = self.place
        swaps = (
            [place.swap_core]
            if self.stage < 0
            else [lambda v, b=o[self.stage]: place.swap(v, b) for o in (self.left, self.right)]
        )
        self.gots = [
            hold(swap(hold(v, *before)), *during) for v, swap in zip(self.sends, swaps)
        ]
        self.stage += 1
        if self.stage == len(self.left):
            self.result = self.keeps[0][0].astype(jnp.float32) + self.gots[0][0].astype(jnp.float32)
        return self.gots


def weight_terms(place, lefts, rights, rows):
    chips = place.chips
    count = len(lefts)
    length, features = lefts[0].shape
    joined = not isinstance(rights, list)
    width = rights.shape[1] // count if joined else rights[0].shape[1]
    per = count // 2
    unique = []
    for l in lefts:
        if not any(l is u for u in unique):
            unique.append(l)
    which = [next(i for i, u in enumerate(unique) if u is l) for l in lefts]
    rights = [rights] if joined else rights

    def body(at, *refs):
        ins, (keep, send) = refs[:-2], refs[-2:]
        t = pl.program_id(0)
        chip, core = at[0], at[1]

        def one(left, right):
            total = lax.dot_general(
                left[...], right[...], (((0,), (0,)), ((), ())), preferred_element_type=jnp.float32
            )
            for c in range(chips):
                to = c ^ chip
                a = total[2 * c * rows : (2 * c + 1) * rows].astype(LOW)
                b = total[(2 * c + 1) * rows : (2 * c + 2) * rows].astype(LOW)
                keep[0, to] = jnp.where(core == 0, a, b)
                send[0, to] = jnp.where(core == 0, b, a)

        if joined:
            one(ins[0], ins[1])
        else:
            for k in range(count):
                pl.when(t == k)(lambda k=k: one(ins[which[k]], ins[len(unique) + k]))

    block = pl.BlockSpec((1, chips, rows, width), lambda t, at: (t // per, 0, 0, t % per))
    shape = jax.ShapeDtypeStruct((2, chips, rows, width * per), LOW)
    fixed = pl.BlockSpec((length, width), lambda t, at: (0, 0))
    return kernel_call(
        body,
        (count,),
        [pl.BlockSpec((length, features), lambda t, at: (0, 0)) for _ in unique]
        + ([pl.BlockSpec((length, width), lambda t, at: (0, t))] if joined else [fixed] * count),
        [block, block],
        [shape, shape],
        (2 * count * length * features * width, 4 * count * features * width, 0),
    )(place.where, *unique, *rights)


def weight_terms_tall(place, left, right, rows):
    chips = place.chips
    length, features = left.shape
    width = right.shape[1]
    tiles = 4
    group = chips // tiles

    def body(at, left_ref, right_ref, keep, send):
        chip, core = at[0], at[1]
        total = lax.dot_general(
            left_ref[...], right_ref[...], (((0,), (0,)), ((), ())), preferred_element_type=jnp.float32
        )
        for c in range(group):
            to = c ^ (chip % group)
            a = total[2 * c * rows : (2 * c + 1) * rows].astype(LOW)
            b = total[(2 * c + 1) * rows : (2 * c + 2) * rows].astype(LOW)
            own, other = jnp.where(core == 0, a, b), jnp.where(core == 0, b, a)
            for side in range(2):
                cols = slice(side * (width // 2), (side + 1) * (width // 2))
                keep[side, to] = own[:, cols]
                send[side, to] = other[:, cols]

    block = pl.BlockSpec((2, group, rows, width // 2), lambda t, at: (0, t, 0, 0))
    shape = jax.ShapeDtypeStruct((2, chips, rows, width // 2), LOW)
    return kernel_call(
        body,
        (tiles,),
        [
            pl.BlockSpec((length, features // tiles), lambda t, at: (0, t ^ (at[0] // group))),
            pl.BlockSpec((length, width), lambda t, at: (0, 0)),
        ],
        [block, block],
        [shape, shape],
        (2 * length * features * width, 4 * features * width, 0),
    )(place.where, left, right)


class Total:
    def __init__(self, place, value):
        self.place, self.value = place, value
        self.strides = [0] + place.fast + place.mid + place.slow

    def step(self, before=(), during=()):
        if not self.strides:
            return None
        value = hold(self.value, *before)
        stride = self.strides.pop(0)
        got = hold(self.place.swap(value, stride) if stride else self.place.swap_core(value), *during)
        self.value = value + got
        return got


def attention_forward(place, start, weights, query_bias, value_bias, seqs):
    rows, width = start.shape
    length = rows // seqs
    cols = 4 * HD
    groups = width // cols

    def body(at, start, wq, wk, wv, qb, vb, query, key, value, context, lse):
        x = start[...]
        dot = lambda l, r: jnp.dot(l, r, preferred_element_type=jnp.float32)
        query[...] = (dot(x, wq[...]) + qb[...]).astype(LOW)
        key[...] = dot(x, wk[...]).astype(LOW)
        value[...] = (dot(x, wv[...]) + vb[...]).astype(LOW)
        lane = lax.broadcasted_iota(jnp.int32, (length, 2 * HD), 1)
        for pair in range(2):
            at_cols = slice(pair * 2 * HD, (pair + 1) * 2 * HD)
            q, k = query[:, at_cols], key[:, at_cols]
            v_across = value[:, at_cols].T
            mixed = []
            for h in range(2):
                mine = (lane < HD) if h == 0 else (lane >= HD)
                q_mine = jnp.where(mine, q * jnp.asarray(HD**-0.5, LOW), jnp.zeros_like(q))
                scores = lax.dot_general(
                    k, q_mine, (((1,), (1,)), ((), ())), preferred_element_type=jnp.float32
                )
                most = jnp.max(scores, axis=0, keepdims=True)
                raised = jnp.exp(scores - most)
                total = jnp.sum(raised, axis=0, keepdims=True)
                probs = (raised * (1.0 / total)).astype(LOW)
                mixed.append(dot(v_across[h * HD : (h + 1) * HD], probs))
                lse[0, 0, 2 * pair + h : 2 * pair + h + 1, :] = most + jnp.log(total)
            context[:, at_cols] = jnp.concatenate(mixed, axis=0).T.astype(LOW)

    block = pl.BlockSpec((length, cols), lambda s, g, at: (s, g))
    weight = pl.BlockSpec((width, cols), lambda s, g, at: (0, g))
    bias = pl.BlockSpec((1, cols), lambda s, g, at: (0, g))
    table = jax.ShapeDtypeStruct((rows, width), LOW)
    return kernel_call(
        body,
        (seqs, groups),
        [pl.BlockSpec((length, width), lambda s, g, at: (s, 0)), weight, weight, weight, bias, bias],
        [block] * 4 + [pl.BlockSpec((1, 1, 4, length), lambda s, g, at: (s, g, 0, 0))],
        [pltpu.HBM(table.shape, LOW)] * 3 + [table, jax.ShapeDtypeStruct((seqs, groups, 4, length), jnp.float32)],
        (6 * rows * width * width, 6 * width * width, seqs * groups * 4 * length * length),
    )(place.where, start, *weights, query_bias, value_bias)


def attention_backward(place, query, key, value, grad_context, lse):
    rows, width = query.shape
    seqs, groups, _, length = lse.shape
    cols = 4 * HD

    def body(at, query, key, value, grad, lse, dq, dk, dv, dq_sum, dv_sum):
        dot = lambda l, r: jnp.dot(l, r, preferred_element_type=jnp.float32)
        dot_t = lambda l, r: lax.dot_general(
            l, r, (((1,), (1,)), ((), ())), preferred_element_type=jnp.float32
        )
        lane = lax.broadcasted_iota(jnp.int32, (length, 2 * HD), 1)
        for pair in range(2):
            at_cols = slice(pair * 2 * HD, (pair + 1) * 2 * HD)
            q, k, v, g = query[:, at_cols], key[:, at_cols], value[:, at_cols], grad[:, at_cols]
            k_across = k.T
            dqs, dks, dvs = [], [], []
            for h in range(2):
                mine = (lane < HD) if h == 0 else (lane >= HD)
                none = jnp.zeros_like(q)
                scaled = jnp.where(mine, q * jnp.asarray(HD**-0.5, LOW), none)
                scores = dot_t(k, scaled)
                probs = jnp.exp(scores - lse[0, 0, 2 * pair + h : 2 * pair + h + 1, :])
                grad_probs = dot_t(v, jnp.where(mine, g, none))
                dvs.append(dot(probs.astype(LOW), g))
                inner = jnp.sum(probs * grad_probs, axis=0, keepdims=True)
                grad_scores = (probs * (grad_probs - inner)).astype(LOW)
                dks.append(dot(grad_scores, q))
                dqs.append(dot(k_across[h * HD : (h + 1) * HD], grad_scores))
            scale = HD**-0.5
            dq_low = (jnp.concatenate(dqs, axis=0).T * scale).astype(LOW)
            dk_low = (jnp.where(lane < HD, dks[0], dks[1]) * scale).astype(LOW)
            dv_low = jnp.where(lane < HD, dvs[0], dvs[1]).astype(LOW)
            dq[:, at_cols], dk[:, at_cols], dv[:, at_cols] = dq_low, dk_low, dv_low
            for total, term in ((dq_sum, dq_low), (dv_sum, dv_low)):
                term = jnp.sum(term.astype(jnp.float32), axis=0, keepdims=True)

                @pl.when(pl.program_id(1) == 0)
                def _(total=total, term=term):
                    total[:, at_cols] = term

                @pl.when(pl.program_id(1) > 0)
                def _(total=total, term=term):
                    total[:, at_cols] += term

    block = pl.BlockSpec((length, cols), lambda g, s, at: (s, g))
    total = pl.BlockSpec((1, cols), lambda g, s, at: (0, g))
    table = jax.ShapeDtypeStruct((rows, width), LOW)
    sums = jax.ShapeDtypeStruct((1, width), jnp.float32)
    return kernel_call(
        body,
        (groups, seqs),
        [block] * 4 + [pl.BlockSpec((1, 1, 4, length), lambda g, s, at: (s, g, 0, 0))],
        [block] * 3 + [total] * 2,
        [table] * 3 + [sums] * 2,
        (10 * rows * length * width, 14 * rows * width, rows * length * width // HD),
    )(place.where, query, key, value, grad_context, lse)


def normalised(value):
    centered = value - jnp.mean(value, axis=-1, keepdims=True)
    inverse = lax.rsqrt(jnp.mean(centered * centered, axis=-1, keepdims=True) + 1e-12)
    return centered * inverse, inverse


def normalised_back(grad, unit, inverse, gain):
    inner = grad * gain
    mean = jnp.mean(inner, axis=-1, keepdims=True)
    along = jnp.mean(inner * unit, axis=-1, keepdims=True)
    return (
        inverse * (inner - mean - unit * along),
        jnp.sum(grad * unit, axis=0, keepdims=True),
        jnp.sum(grad, axis=0, keepdims=True),
    )


def feed_in(place, start, context, wo, output_bias, gain, shift, wi, inner_bias):
    rows, width = start.shape
    inner = wi.shape[1]
    tile = width

    def body(at, start, context, wo, ob, gain, shift, wi, ib, unit, inverse, normed_low, active, slope):
        @pl.when(pl.program_id(0) == 0)
        def _():
            first = (
                start[...].astype(jnp.float32)
                + jnp.dot(context[...], wo[...], preferred_element_type=jnp.float32)
                + ob[...]
            )
            u, i = normalised(first)
            unit[...] = u
            inverse[...] = i
            normed_low[...] = (u * gain[...] + shift[...]).astype(LOW)

        for part in range(4):
            cut = slice(part * tile // 4, (part + 1) * tile // 4)
            hidden = (
                jnp.dot(normed_low[...], wi[:, cut], preferred_element_type=jnp.float32) + ib[:, cut]
            )
            below = 0.5 + 0.5 * lax.erf(hidden * 0.7071067811865476)
            active[:, cut] = (hidden * below).astype(LOW)
            bell = jnp.exp(hidden * hidden * -0.5) * 0.3989422804014327
            slope[:, cut] = (below + hidden * bell).astype(LOW)

    keep = lambda a: pl.BlockSpec(a.shape, lambda t, at: (0, 0))
    column = pl.BlockSpec((rows, tile), lambda t, at: (0, t))
    shapes = [
        jax.ShapeDtypeStruct((rows, width), jnp.float32),
        jax.ShapeDtypeStruct((rows, 1), jnp.float32),
        jax.ShapeDtypeStruct((rows, width), LOW),
        jax.ShapeDtypeStruct((rows, inner), LOW),
        jax.ShapeDtypeStruct((rows, inner), LOW),
    ]
    ins = (start, context, wo, output_bias, gain, shift)
    return kernel_call(
        body,
        (inner // tile,),
        [keep(a) for a in ins]
        + [
            pl.BlockSpec((width, tile), lambda t, at: (0, t)),
            pl.BlockSpec((1, tile), lambda t, at: (0, t)),
        ],
        [keep(s) for s in shapes[:3]] + [column, column],
        shapes,
        (2 * rows * width * (width + inner), 2 * width * inner, 2 * rows * inner),
    )(place.where, *ins, wi, inner_bias)


def feed_out(place, active, wu, outer_bias, unit, gain_one, shift_one, gain, shift, cotangent, wanted):
    rows, width = unit.shape
    inner = active.shape[1]
    tile = width
    steps = inner // tile

    def body(at, active, wu, ob, unit, g1, s1, g2, s2, cot, wanted, out, grad, branch, ob_g, g2_g, s2_g, total):
        t = pl.program_id(0)
        term = jnp.dot(active[...], wu[...], preferred_element_type=jnp.float32)

        @pl.when(t == 0)
        def _():
            total[...] = unit[...] * g1[...] + s1[...] + ob[...] + term

        @pl.when(t > 0)
        def _():
            total[...] += term

        @pl.when(t == steps - 1)
        def _():
            u, i = normalised(total[...])
            out[...] = (u * g2[...] + s2[...]).astype(LOW)
            grad_out = cot[...].astype(jnp.float32) * wanted[...]
            back, gain_grad, shift_grad = normalised_back(grad_out, u, i, g2[...])
            grad[...] = back
            low = back.astype(LOW)
            branch[...] = low
            ob_g[...] = jnp.sum(low.astype(jnp.float32), axis=0, keepdims=True)
            g2_g[...] = gain_grad
            s2_g[...] = shift_grad

    keep = lambda a: pl.BlockSpec(a.shape, lambda t, at: (0, 0))
    row = jax.ShapeDtypeStruct((1, width), jnp.float32)
    shapes = [
        jax.ShapeDtypeStruct((rows, width), LOW),
        jax.ShapeDtypeStruct((rows, width), jnp.float32),
        jax.ShapeDtypeStruct((rows, width), LOW),
        row,
        row,
        row,
    ]
    ins = (outer_bias, unit, gain_one, shift_one, gain, shift, cotangent, wanted)
    return kernel_call(
        body,
        (steps,),
        [
            pl.BlockSpec((rows, tile), lambda t, at: (0, t)),
            pl.BlockSpec((tile, width), lambda t, at: (t, 0)),
        ]
        + [keep(a) for a in ins],
        [keep(s) for s in shapes],
        shapes,
        (2 * rows * width * inner, 2 * width * inner, 0),
        [pltpu.VMEM((rows, width), jnp.float32)],
    )(place.where, active, wu, *ins)


def hidden_back(place, grad_branch, wu, slope):
    rows, width = grad_branch.shape
    inner = wu.shape[0]
    tile = width

    def body(at, grad, wu, slope, out, sums):
        back = lax.dot_general(
            grad[...], wu[...], (((1,), (1,)), ((), ())), preferred_element_type=jnp.float32
        )
        low = (back * slope[...].astype(jnp.float32)).astype(LOW)
        out[...] = low
        sums[...] = jnp.sum(low.astype(jnp.float32), axis=0, keepdims=True)

    column = pl.BlockSpec((rows, tile), lambda t, at: (0, t))
    return kernel_call(
        body,
        (inner // tile,),
        [
            pl.BlockSpec((rows, width), lambda t, at: (0, 0)),
            pl.BlockSpec((tile, width), lambda t, at: (t, 0)),
            column,
        ],
        [column, pl.BlockSpec((1, tile), lambda t, at: (0, t))],
        [jax.ShapeDtypeStruct((rows, inner), LOW), jax.ShapeDtypeStruct((1, inner), jnp.float32)],
        (2 * rows * width * inner, 2 * width * inner, 0),
    )(place.where, grad_branch, wu, slope)


def first_back(place, grad_hidden, wi, grad_second, unit, inverse, gain, wo):
    rows, width = grad_second.shape
    inner = wi.shape[1]
    tile = width
    steps = inner // tile

    def body(at, gh, wi, second, unit, inverse, gain, wo, first, low_out, context, ob_g, g_g, s_g, total):
        t = pl.program_id(0)
        term = lax.dot_general(
            gh[...], wi[...], (((1,), (1,)), ((), ())), preferred_element_type=jnp.float32
        )

        @pl.when(t == 0)
        def _():
            total[...] = second[...] + term

        @pl.when(t > 0)
        def _():
            total[...] += term

        @pl.when(t == steps - 1)
        def _():
            back, gain_grad, shift_grad = normalised_back(
                total[...], unit[...], inverse[...], gain[...]
            )
            first[...] = back
            low = back.astype(LOW)
            low_out[...] = low
            ob_g[...] = jnp.sum(low.astype(jnp.float32), axis=0, keepdims=True)
            g_g[...] = gain_grad
            s_g[...] = shift_grad
            context[...] = lax.dot_general(
                low, wo[...], (((1,), (1,)), ((), ())), preferred_element_type=jnp.float32
            ).astype(LOW)

    keep = lambda a: pl.BlockSpec(a.shape, lambda t, at: (0, 0))
    row = jax.ShapeDtypeStruct((1, width), jnp.float32)
    shapes = [
        jax.ShapeDtypeStruct((rows, width), jnp.float32),
        jax.ShapeDtypeStruct((rows, width), LOW),
        jax.ShapeDtypeStruct((rows, width), LOW),
        row,
        row,
        row,
    ]
    ins = (grad_second, unit, inverse, gain, wo)
    return kernel_call(
        body,
        (steps,),
        [
            pl.BlockSpec((rows, tile), lambda t, at: (0, t)),
            pl.BlockSpec((width, tile), lambda t, at: (0, t)),
        ]
        + [keep(a) for a in ins],
        [keep(s) for s in shapes],
        shapes,
        (2 * rows * width * (inner + width), 2 * width * inner, 0),
        [pltpu.VMEM((rows, width), jnp.float32)],
    )(place.where, grad_hidden, wi, *ins)


def start_back(place, grad_first, grads, weights, masked):
    rows, width = grad_first.shape

    def body(at, first, dq, dk, dv, wq, wk, wv, masked, out, sums):
        total = first[...]
        for grad, weight in ((dq, wq), (dk, wk), (dv, wv)):
            total += lax.dot_general(
                grad[...], weight[...], (((1,), (1,)), ((), ())), preferred_element_type=jnp.float32
            )
        hidden = masked[...] > 0.0
        out[...] = jnp.where(hidden, 0.0, total).astype(LOW)
        sums[...] = jnp.sum(jnp.where(hidden, total, 0.0), axis=0, keepdims=True)

    ins = (grad_first, *grads, *weights, masked)
    shapes = [jax.ShapeDtypeStruct((rows, width), LOW), jax.ShapeDtypeStruct((1, width), jnp.float32)]
    return kernel_call(
        body,
        (1,),
        [pl.BlockSpec(a.shape, lambda t, at: (0, 0)) for a in ins],
        [pl.BlockSpec(s.shape, lambda t, at: (0, 0)) for s in shapes],
        shapes,
        (6 * rows * width * width, 6 * width * width, 0),
    )(place.where, *ins)


class PlainGather:
    def __init__(self, rows):
        self.rows = rows
        self.ready = ()

    def step(self, before=(), during=()):
        return None

    def done(self, parts):
        whole = lax.all_gather(self.rows, BOTH, axis=0, tiled=True)
        half = whole.shape[1] // 2
        outs, begin = [], 0
        for width in parts:
            outs.append(
                jnp.concatenate(
                    [whole[:, s * half + begin : s * half + begin + width] for s in range(2)], axis=1
                )
            )
            begin += width
        return outs


class PlainScatter:
    def __init__(self, term):
        self.result = lax.psum_scatter(term, BOTH, scatter_dimension=0, tiled=True)
        self.sends = ()

    def fold(self):
        return ()

    def send(self, before=(), during=()):
        return ()


class PlainTotal:
    def __init__(self, value):
        self.value = lax.psum(value, BOTH)

    def step(self, before=(), during=()):
        return None


def outer_sum(left, right):
    return jnp.einsum("rd,re->de", left, right, preferred_element_type=jnp.float32)


def halves(place, arrays):
    spots, column = [], 0
    for side in range(2):
        for i, a in enumerate(arrays):
            half = a.shape[1] // 2
            spots.append((i, side * half, half, 0, column))
            column += half
    return pack(place, arrays, spots, (arrays[0].shape[0], column))


def on_device(
    tokens,
    span_starts,
    span_lengths,
    mask_embed,
    query_weight,
    key_weight,
    value_weight,
    output_weight,
    inner_weight,
    outer_weight,
    query_bias,
    value_bias,
    output_bias,
    inner_bias,
    outer_bias,
    gain_one,
    shift_one,
    gain_two,
    shift_two,
    cotangent,
):
    rows, width = tokens.shape
    seqs = span_starts.shape[0]
    length = rows // seqs
    inner = inner_weight.shape[1]
    own_rows, own_tall = query_weight.shape[0], outer_weight.shape[0]
    place = Place()
    staged = own_rows % 8 == 0 and place.chips & (place.chips - 1) == 0
    gather = (lambda piece: Gather(place, piece)) if staged else PlainGather

    first_gather = gather(halves(place, (query_weight, key_weight, value_weight)))
    inner_gather = gather(halves(place, (output_weight, inner_weight)))
    outer_gather = gather(outer_weight)
    first_gather.step()
    places = jnp.arange(length, dtype=jnp.int32)[None, :, None]
    begins = span_starts[:, None, :]
    finish = begins + span_lengths[:, None, :]
    masked = jnp.any((places >= begins) & (places < finish), axis=2)
    edges = jnp.any((places == begins - 1) | (places == finish), axis=2)
    masked = masked.reshape(rows)
    wanted = (masked | edges.reshape(rows)).astype(jnp.float32)[:, None]
    start = jnp.where(masked[:, None], mask_embed[None, :], tokens)
    masked = masked.astype(jnp.float32)[:, None]
    vectors = (
        query_bias,
        value_bias,
        output_bias,
        inner_bias,
        outer_bias,
        gain_one,
        shift_one,
        gain_two,
        shift_two,
    )
    vectors = tuple(v[None] for v in vectors)
    query_row, value_row, output_row, inner_row, outer_row, gain_1, shift_1, gain_2, shift_2 = vectors
    before = first_gather.ready
    first_gather.step(during=(*vectors, start, masked, wanted))
    inner_gather.step(before, first_gather.ready)
    before = first_gather.ready
    first_gather.step()
    inner_gather.step(before, first_gather.ready)
    first_gather.step()
    before = inner_gather.ready
    inner_gather.step(first_gather.ready)
    outer_gather.step(before, inner_gather.ready)
    got = first_gather.step()
    weights = first_gather.done((width // 2,) * 3)
    query, key, value, context, lse = attention_forward(
        place, hold(start, *inner_gather.ready, *outer_gather.ready), weights, query_row, value_row, seqs
    )
    outer_gather.step(inner_gather.ready, (context,))
    inner_gather.step((got,), (context, *outer_gather.ready))
    got = inner_gather.step((context,))
    outer_gather.step(inner_gather.ready, (got,))
    wo, wi = inner_gather.done((width // 2, inner // 2))
    unit, inverse, normed_low, active, slope = feed_in(
        place, start, hold(context, *outer_gather.ready), wo, output_row, gain_1, shift_1, wi, inner_row
    )
    outer_gather.step((), (active,))
    outer_gather.step()
    (wu,) = outer_gather.done((width // 2,))
    layer_output, grad_second, grad_branch, outer_bias_grad, gain_two_grad, shift_two_grad = feed_out(
        place, active, wu, outer_row, unit, gain_1, shift_1, gain_2, shift_2, cotangent, wanted
    )
    if staged:
        outer_sums = Scatter(place, *weight_terms_tall(place, active, grad_branch, own_tall))
    else:
        outer_sums = PlainScatter(outer_sum(active, grad_branch))
    grad_hidden, inner_bias_grad = hidden_back(place, hold(grad_branch, *outer_sums.sends), wu, slope)
    outer_sums.send((), (grad_hidden,))
    outer_sums.fold()
    if staged:
        tiles = inner // width
        grad_tied = hold(grad_hidden, *outer_sums.sends)
        inner_sums = Scatter(place, *weight_terms(place, [normed_low] * tiles, grad_tied, own_rows))
    else:
        inner_sums = PlainScatter(outer_sum(normed_low, grad_hidden))
    outer_sums.send((), inner_sums.sends)
    outer_sums.fold()
    tied = hold(grad_hidden, *inner_sums.sends, *outer_sums.sends)
    grad_first, grad_attended, grad_context, output_bias_grad, gain_one_grad, shift_one_grad = first_back(
        place, tied, wi, grad_second, unit, inverse, gain_1, wo
    )
    outer_sums.send((), (grad_context,))
    inner_sums.send((), (grad_context,))
    inner_sums.fold()
    outer_sums.fold()
    tied = hold(grad_context, *outer_sums.sends, *inner_sums.sends)
    grad_query, grad_key, grad_value, query_bias_grad, value_bias_grad = attention_backward(
        place, query, key, value, tied, lse
    )
    inner_sums.send((), (grad_query,))
    outer_sums.send((), (grad_query,))
    inner_sums.fold()
    outer_sums.fold()
    lefts = [start, start, start, context]
    rights = [hold(grad_query, *outer_sums.sends, *inner_sums.sends), grad_key, grad_value, grad_attended]
    if staged:
        first_sums = Scatter(place, *weight_terms(place, lefts, rights, own_rows))
    else:
        first_sums = PlainScatter(
            jnp.concatenate([outer_sum(l, r) for l, r in zip(lefts, rights)], axis=1)
        )
    inner_sums.send((), first_sums.sends)
    outer_sums.send((), first_sums.sends)
    inner_sums.fold()
    grad_query = hold(grad_query, *first_sums.sends, *inner_sums.sends)
    input_grad, mask_grad = start_back(
        place, grad_first, (grad_query, grad_key, grad_value), weights, masked
    )
    first_sums.send((), (mask_grad,))
    first_sums.fold()
    tied = (mask_grad, *first_sums.sends)
    late = inner_sums.send((), tied)
    inner_sums.fold()
    smalls = (
        query_bias_grad,
        value_bias_grad,
        output_bias_grad,
        outer_bias_grad,
        gain_one_grad,
        shift_one_grad,
        gain_two_grad,
        shift_two_grad,
        mask_grad,
        inner_bias_grad,
    )
    spots = [(i, 0, width, i, 0) for i in range(9)]
    spots += [(9, i * width, width, 9 + i, 0) for i in range(inner // width)]
    high = -(-(9 + inner // width) // 8) * 8
    smalls = (hold(query_bias_grad, *inner_sums.sends), *smalls[1:])
    packed = pack(place, smalls, spots, (high, width))
    total = Total(place, packed) if staged else PlainTotal(packed)
    got = total.step(first_sums.sends)
    got = total.step(first_sums.sends)
    late = inner_sums.send(first_sums.sends)
    first_sums.send((), (got, *late))
    first_sums.fold()
    got = total.step(first_sums.sends)
    first_sums.send((), (got,))
    first_sums.fold()
    got = total.step(first_sums.sends)
    first_sums.send((), (got,))
    first_sums.fold()
    total.step(first_sums.sends)
    first_sums.send()
    packed = total.value
    order = (0, 1, 2, 9, 3, 4, 5, 6, 7, 8)
    firsts = first_sums.result
    return (
        layer_output,
        input_grad,
        *(firsts[:, i * width : (i + 1) * width] for i in range(4)),
        inner_sums.result,
        outer_sums.result,
        *(packed[9:9 + inner // width].reshape(-1) if i == 9 else packed[i] for i in order),
    )


def solution(mesh):
    placed = (
        P(("dp", "pair"), None),
        P(("dp", "pair"), None),
        P(("dp", "pair"), None),
        P(),
        P(("dp", "pair"), None),
        P(("dp", "pair"), None),
        P(("dp", "pair"), None),
        P(("dp", "pair"), None),
        P(("dp", "pair"), None),
        P(("dp", "pair"), None),
        P(),
        P(),
        P(),
        P(),
        P(),
        P(),
        P(),
        P(),
        P(),
        P(("dp", "pair"), None),
    )
    return jax.shard_map(
        on_device,
        mesh=mesh,
        in_specs=placed,
        out_specs=(
            P(("dp", "pair"), None),
            P(("dp", "pair"), None),
            P(("dp", "pair"), None),
            P(("dp", "pair"), None),
            P(("dp", "pair"), None),
            P(("dp", "pair"), None),
            P(("dp", "pair"), None),
            P(("dp", "pair"), None),
            P(),
            P(),
            P(),
            P(),
            P(),
            P(),
            P(),
            P(),
            P(),
            P(),
        ),
        check_vma=False,
    )
```
